32 devices in a mesh: sx: 8 (over y, x, core), sy: 4 (over z).
Axes of the slice: x: 2, y: 2, z: 4, core: 2. Of those that a mesh axis runs over, the one named last changes fastest.
Arguments:
- schur_x: float32 [16, 4, 512, 512], P('sx', 'sy'), may hold values from -1 to 5, as said below
- schur_y: float32 [8, 8, 512, 512], P('sx', 'sy'), may hold values from -1 to 5, as said below
- residual_x: float32 [16, 4, 32, 512], P('sx', 'sy'), may hold values from -36 to 36
- residual_y: float32 [8, 8, 32, 512], P('sx', 'sy'), may hold values from -36 to 36
- basis_x: float32 [16, 4, 6, 512], P('sx', 'sy'), may hold values from -0.9 to 0.9
- basis_y: float32 [8, 8, 6, 512], P('sx', 'sy'), may hold values from -0.9 to 0.9
- couple_x: float32 [8, 4, 6, 6], P('sx', 'sy'), may hold values from -0.3 to 0.1
- couple_y: float32 [8, 4, 6, 6], P('sx', 'sy'), may hold values from -0.3 to 0.1
- coarse_shift: float32 [8, 4, 6], P('sx', 'sy'), may hold values from 0.05 to 0.5
Outputs:
- average_x: float32 [16, 4, 32, 512], P('sx', 'sy')
- average_y: float32 [8, 8, 32, 512], P('sx', 'sy')
- coarse_values: float32 [8, 4, 6, 32], P('sx', 'sy')
The draws below stay inside these ranges and needn't reach their ends.
Inputs may be any that keep to these rules, and one draw needn't show every extreme that they name: `schur_x`: every block is symmetric positive definite. `schur_y`: every block is symmetric positive definite.
All inputs are finite; a program needn't handle non-finite values.
Results may differ from the reference program's by a relative error of at most 0.0003.
Values sent between devices are 32-bit elements; how exact they have to be, the bound alone decides.
No kernel may reach another device: no remote copies, remote signals or barrier semaphores. Data moves between devices by JAX's collectives and lax.ppermute only.
A program may use at most 128 MiB of HBM per device.

```python
import math
import jax
import jax.numpy as jnp
from jax import lax

F = 512
R = 32
PC = 6
CITERS = 8
SUBX = 8
SUBY = 4


def make_blocks(key, count):
    keys = jax.random.split(key, count)

    def single(subkey):
        first_key, second_key, third_key = jax.random.split(subkey, 3)
        factor = jnp.clip(jax.random.normal(first_key, (F, F), jnp.float32), -4.0, 4.0)
        spread = jnp.exp(jax.random.uniform(second_key, (F,), jnp.float32, math.log(0.003), math.log(0.03)))
        weights = jnp.exp(jax.random.uniform(third_key, (F,), jnp.float32, math.log(0.001), math.log(2.0)))
        product = jnp.dot(factor * weights[None, :], factor.T, precision=lax.Precision.HIGHEST)
        return product / F + jnp.diag(spread)
    return lax.map(single, keys)


def make_residual(key, rows, cols, position):
    first_key, second_key = jax.random.split(key, 2)
    base = jnp.clip(jax.random.normal(first_key, (rows, cols, R, F), jnp.float32), -6.0, 6.0)
    device_scale = jnp.exp(jax.random.uniform(second_key, (rows, cols, 1, 1), jnp.float32, 0.0, math.log(2.0)))
    growth = jnp.exp(position * math.log(3.0))
    return base * device_scale * growth


def draw_schur_x(key, part):
    return make_blocks(key, 2 * SUBX * SUBY).reshape(2 * SUBX, SUBY, F, F)


def draw_schur_y(key, part):
    return make_blocks(key, 2 * SUBX * SUBY).reshape(SUBX, 2 * SUBY, F, F)


def draw_residual_x(key, part):
    position = (jnp.arange(2 * SUBX) // 2).astype(jnp.float32) / (SUBX - 1)
    return make_residual(key, 2 * SUBX, SUBY, position[:, None, None, None])


def draw_residual_y(key, part):
    position = jnp.arange(SUBX).astype(jnp.float32) / (SUBX - 1)
    return make_residual(key, SUBX, 2 * SUBY, position[:, None, None, None])


def levels(own_key, extent, shards, least, high):
    loudness = 1.0
    for dim, parts in shards:
        steps = jax.random.uniform(jax.random.fold_in(jax.random.fold_in(own_key, 6), dim), (parts,), jnp.float32, least / len(shards), high / len(shards))
        loudness = loudness * jnp.repeat(jnp.exp(steps), extent[dim] // parts).reshape((-1,) + (1,) * (len(extent) - 1 - dim))
    return loudness


def gaussian(own_key, dims, scale, limit, pieces=(), held_as=jnp.bfloat16):
    result = scale * jax.random.normal(own_key, dims, jnp.float32)
    if pieces:
        result = result * levels(own_key, dims, pieces, -0.22, 0.18)
    return jnp.clip(result, -limit, limit).astype(held_as)


def setup_inputs(seed: int = 0) -> dict:
    key_of = jax.random.split(jax.random.key(seed), 10)
    schur_x = draw_schur_x(jax.random.fold_in(key_of[9], 71), 0)
    schur_y = draw_schur_y(jax.random.fold_in(key_of[9], 71), 0)
    residual_x = draw_residual_x(jax.random.fold_in(key_of[9], 71), 0)
    residual_y = draw_residual_y(jax.random.fold_in(key_of[9], 71), 0)
    basis_x = gaussian(key_of[4], (2 * SUBX, SUBY, PC, F), 0.15, 0.9, ((0, 8), (1, 4)), jnp.float32)
    basis_y = gaussian(key_of[5], (SUBX, 2 * SUBY, PC, F), 0.15, 0.9, ((0, 8), (1, 4)), jnp.float32)
    couple_x = jnp.clip(-0.3 + 0.4 * jax.random.uniform(key_of[6], (SUBX, SUBY, PC, PC), jnp.float32) ** levels(key_of[6], (SUBX, SUBY, PC, PC), ((0, 8), (1, 4)), -0.2, 0.2), -0.3, 0.1)
    couple_y = jnp.clip(-0.3 + 0.4 * jax.random.uniform(key_of[7], (SUBX, SUBY, PC, PC), jnp.float32) ** levels(key_of[7], (SUBX, SUBY, PC, PC), ((0, 8), (1, 4)), -0.2, 0.2), -0.3, 0.1)
    coarse_shift = jnp.clip(jnp.exp(math.log(0.5) - 2.3025851 * jax.random.uniform(key_of[8], (SUBX, SUBY, PC), jnp.float32) ** levels(key_of[8], (SUBX, SUBY, PC), ((0, 8), (1, 4)), -0.2, 0.2)), 0.05, 0.5)
    return dict(schur_x=schur_x, schur_y=schur_y, residual_x=residual_x, residual_y=residual_y, basis_x=basis_x, basis_y=basis_y, couple_x=couple_x, couple_y=couple_y, coarse_shift=coarse_shift)


HIGH = lax.Precision.HIGHEST

def face_average(s_low, s_high, r_low, r_high):
    summed = s_low + s_high
    factor = jnp.linalg.cholesky(summed)
    right_side = jnp.dot(s_low, r_low.T, precision=HIGH) + jnp.dot(s_high, r_high.T, precision=HIGH)
    forward = jax.scipy.linalg.solve_triangular(factor, right_side, lower=True)
    solved = jax.scipy.linalg.solve_triangular(factor, forward, lower=True, trans=1)
    return solved.T

def reference(schur_x, schur_y, residual_x, residual_y, basis_x, basis_y, couple_x, couple_y, coarse_shift):
    blocks_x = schur_x.reshape(SUBX, 2, SUBY, F, F)
    resid_bx = residual_x.reshape(SUBX, 2, SUBY, R, F)
    basis_bx = basis_x.reshape(SUBX, 2, SUBY, PC, F)
    blocks_y = schur_y.reshape(SUBX, SUBY, 2, F, F)
    resid_by = residual_y.reshape(SUBX, SUBY, 2, R, F)
    basis_by = basis_y.reshape(SUBX, SUBY, 2, PC, F)

    def pair_x(index):
        row_pos = index // SUBY
        col_pos = index % SUBY
        return face_average(blocks_x[row_pos, 1, col_pos], blocks_x[row_pos + 1, 0, col_pos], resid_bx[row_pos, 1, col_pos], resid_bx[row_pos + 1, 0, col_pos])

    def pair_y(index):
        row_pos = index // (SUBY - 1)
        col_pos = index % (SUBY - 1)
        return face_average(blocks_y[row_pos, col_pos, 1], blocks_y[row_pos, col_pos + 1, 0], resid_by[row_pos, col_pos, 1], resid_by[row_pos, col_pos + 1, 0])
    faces_x = lax.map(pair_x, jnp.arange((SUBX - 1) * SUBY, dtype=jnp.int32)).reshape(SUBX - 1, SUBY, R, F)
    faces_y = lax.map(pair_y, jnp.arange(SUBX * (SUBY - 1), dtype=jnp.int32)).reshape(SUBX, SUBY - 1, R, F)
    lower_x = jnp.concatenate([resid_bx[:1, 0], faces_x], axis=0)
    upper_x = jnp.concatenate([faces_x, resid_bx[-1:, 1]], axis=0)
    lower_y = jnp.concatenate([resid_by[:, :1, 0], faces_y], axis=1)
    upper_y = jnp.concatenate([faces_y, resid_by[:, -1:, 1]], axis=1)
    rhs_coarse = jnp.einsum('isjpf,isjrf->ijpr', basis_bx, resid_bx, precision=HIGH)
    rhs_coarse = rhs_coarse + jnp.einsum('ijspf,ijsrf->ijpr', basis_by, resid_by, precision=HIGH)
    mask_x = (jnp.arange(SUBX, dtype=jnp.int32) > 0).astype(jnp.float32)
    mask_y = (jnp.arange(SUBY, dtype=jnp.int32) > 0).astype(jnp.float32)
    link_x = couple_x * mask_x[:, None, None, None]
    link_y = couple_y * mask_y[None, :, None, None]
    next_x = jnp.concatenate([link_x[1:], jnp.zeros((1, SUBY, PC, PC), jnp.float32)], axis=0)
    next_y = jnp.concatenate([link_y[:, 1:], jnp.zeros((SUBX, 1, PC, PC), jnp.float32)], axis=1)
    diagonal = jnp.sum(jnp.abs(link_x), axis=2) + jnp.sum(jnp.abs(next_x), axis=3) + jnp.sum(jnp.abs(link_y), axis=2) + jnp.sum(jnp.abs(next_y), axis=3) + coarse_shift

    def operate(field):
        zero_x = jnp.zeros((1, SUBY, PC, R), jnp.float32)
        zero_y = jnp.zeros((SUBX, 1, PC, R), jnp.float32)
        prev_fx = jnp.concatenate([zero_x, field[:-1]], axis=0)
        next_fx = jnp.concatenate([field[1:], zero_x], axis=0)
        prev_fy = jnp.concatenate([zero_y, field[:, :-1]], axis=1)
        next_fy = jnp.concatenate([field[:, 1:], zero_y], axis=1)
        image = diagonal[..., None] * field
        image = image + jnp.einsum('ijab,ijar->ijbr', link_x, prev_fx, precision=HIGH)
        image = image + jnp.einsum('ijab,ijbr->ijar', next_x, next_fx, precision=HIGH)
        image = image + jnp.einsum('ijab,ijar->ijbr', link_y, prev_fy, precision=HIGH)
        image = image + jnp.einsum('ijab,ijbr->ijar', next_y, next_fy, precision=HIGH)
        return image
    coarse = jnp.zeros_like(rhs_coarse)
    remain = rhs_coarse
    direction = rhs_coarse
    norm_now = jnp.sum(remain * remain, axis=(0, 1, 2))
    for sweep_index in range(CITERS):
        image = operate(direction)
        alpha = norm_now / jnp.sum(direction * image, axis=(0, 1, 2))
        coarse = coarse + alpha * direction
        remain = remain - alpha * image
        norm_next = jnp.sum(remain * remain, axis=(0, 1, 2))
        direction = remain + norm_next / norm_now * direction
        norm_now = norm_next
    out_x = jnp.stack([lower_x, upper_x], axis=1)
    out_x = out_x + jnp.einsum('ijpr,isjpf->isjrf', coarse, basis_bx, precision=HIGH)
    out_y = jnp.stack([lower_y, upper_y], axis=2)
    out_y = out_y + jnp.einsum('ijpr,ijspf->ijsrf', coarse, basis_by, precision=HIGH)
    return (out_x.reshape(2 * SUBX, SUBY, R, F), out_y.reshape(SUBX, 2 * SUBY, R, F), coarse)
```

```python
import jax
import jax.numpy as jnp
from jax import lax
from jax.experimental import pallas as pl
from jax.experimental.pallas import tpu as pltpu
from jax.sharding import PartitionSpec as P

CITERS = 8
TILE = 8
BLOCK = 128

HIGH = lax.Precision.HIGHEST


def shifted(array, axis, by):
    count = lax.axis_size(axis)
    pairs = [(i, i + by) for i in range(count) if 0 <= i + by < count]
    return lax.ppermute(array, axis, pairs)


def nt_dot(left, right):
    return lax.dot_general(
        left, right, (((1,), (1,)), ((), ())), precision=HIGH, preferred_element_type=jnp.float32
    )


def nn_dot(left, right):
    return jnp.dot(left, right, precision=HIGH, preferred_element_type=jnp.float32)


def lane_spread(tile, k):
    return jnp.broadcast_to(tile[:, k : k + 1], tile.shape)


def row_spread(tile, k):
    return jnp.broadcast_to(tile[k : k + 1, :], tile.shape)


def inverse_factors(tiles):
    faces = range(len(tiles))
    tiles = [list(rows) for rows in tiles]
    count = len(tiles[0])
    shape = tiles[0][0].shape
    lane = lax.broadcasted_iota(jnp.int32, shape, 1)
    sub = lax.broadcasted_iota(jnp.int32, shape, 0)
    result = [[None] * count for _ in faces]
    for p in range(count):
        base = TILE * p
        cols = [[lane_spread(tiles[f][p], base + j) for j in range(TILE)] for f in faces]
        rows = [tiles[f][p] for f in faces]
        pivot_rows, pivots, inverses = {}, {}, {}
        for k in range(TILE):
            here = sub == k
            column = lane == base + k
            for f in faces:
                pivot = row_spread(cols[f][k], k)
                inverse = 1.0 / pivot
                pivot_row = jnp.where(column, 1.0, row_spread(rows[f], k))
                if k == 0:
                    pivot_rows[f], pivots[f], inverses[f] = pivot_row, pivot, inverse
                else:
                    later = sub >= k
                    pivot_rows[f] = jnp.where(later, pivot_row, pivot_rows[f])
                    pivots[f] = jnp.where(later, pivot, pivots[f])
                    inverses[f] = jnp.where(later, inverse, inverses[f])
                factor = jnp.where(here, 0.0, cols[f][k] * inverse)
                for j in range(k + 1, TILE):
                    cols[f][j] = cols[f][j] - factor * row_spread(cols[f][j], k)
                unit = jnp.where(here, 1.0, 0.0)
                rows[f] = jnp.where(column, unit, rows[f]) - factor * pivot_row
        for f in faces:
            scaled = pivot_rows[f] * lax.rsqrt(pivots[f])
            result[f][p] = jnp.where(lane <= base + sub, scaled, 0.0)
        inside = (lane >= base) & (lane < base + TILE)
        for f in faces:
            reduced = rows[f] * inverses[f]
            spread = [row_spread(reduced, j) for j in range(TILE)]
            for i in range(p + 1, count):
                tile = tiles[f][i]
                terms = [lane_spread(tile, base + j) * spread[j] for j in range(TILE)]
                while len(terms) > 1:
                    terms = [terms[t] + terms[t + 1] for t in range(0, len(terms), 2)]
                tiles[f][i] = jnp.where(inside, 0.0, tile) - terms[0]
    return result


def face_kernel(
    own_x, own_y, far_x, far_y, res_x, res_y, far_res_x, far_res_y, out_x, out_y, work, inv
):
    size = far_x.shape[0]
    cols = res_x.shape[-2]
    blocks = size // BLOCK
    faces = ((own_x, far_x, res_x, far_res_x, out_x), (own_y, far_y, res_y, far_res_y, out_y))
    for f, (own, far, res, far_res, _) in enumerate(faces):
        for k in range(blocks):
            lo = k * BLOCK
            work[f, lo:size, lo : lo + BLOCK] = (
                own[0, 0, lo:size, lo : lo + BLOCK] + far[lo:size, lo : lo + BLOCK]
            )
        work[f, size:, :] = nt_dot(res[0, 0], own[0, 0]) + nt_dot(far_res[...], far[...])

    def diagonal(k, carry):
        lo = pl.multiple_of(k * BLOCK, BLOCK)
        tiles = [
            [work[f, pl.ds(lo + TILE * i, TILE), pl.ds(lo, BLOCK)] for i in range(BLOCK // TILE)]
            for f in range(2)
        ]
        made = inverse_factors(tiles)
        for f in range(2):
            for i in range(BLOCK // TILE):
                inv[f, k, TILE * i : TILE * i + TILE, :] = made[f][i]
        return carry

    for k in range(blocks):
        diagonal(k, 0)
        lo = k * BLOCK
        hi = lo + BLOCK
        for f in range(2):
            panel = nt_dot(work[f, hi:, lo:hi], inv[f, k])
            work[f, hi:, lo:hi] = panel
            for j in range(k + 1, blocks):
                at = j * BLOCK
                work[f, at:, at : at + BLOCK] = work[f, at:, at : at + BLOCK] - nt_dot(
                    panel[at - hi :], panel[at - hi : at - hi + BLOCK]
                )
    for f, (_, _, _, _, out) in enumerate(faces):
        solved = {}
        for k in reversed(range(blocks)):
            lo = k * BLOCK
            hi = lo + BLOCK
            value = work[f, size:, lo:hi]
            for j in range(k + 1, blocks):
                value = value - nn_dot(solved[j], work[f, j * BLOCK : (j + 1) * BLOCK, lo:hi])
            solved[k] = nn_dot(value, inv[f, k])
            out[:, lo:hi] = solved[k]


def solve_faces(schur_x, schur_y, far_x, far_y, res_x, res_y, far_res_x, far_res_y):
    size = schur_x.shape[-1]
    cols = res_x.shape[-2]
    upper_x = lambda i: (1, 0, 0, 0)
    upper_y = lambda i: (0, 1, 0, 0)
    whole = lambda i: (0, 0)
    square = (1, 1, size, size)
    slab = (1, 1, cols, size)
    shape = jax.ShapeDtypeStruct((cols, size), jnp.float32)
    return pl.pallas_call(
        face_kernel,
        grid=(1,),
        in_specs=[
            pl.BlockSpec(square, upper_x),
            pl.BlockSpec(square, upper_y),
            pl.BlockSpec((size, size), whole),
            pl.BlockSpec((size, size), whole),
            pl.BlockSpec(slab, upper_x),
            pl.BlockSpec(slab, upper_y),
            pl.BlockSpec((cols, size), whole),
            pl.BlockSpec((cols, size), whole),
        ],
        out_specs=[pl.BlockSpec((cols, size), whole)] * 2,
        out_shape=[shape, shape],
        scratch_shapes=[
            pltpu.VMEM((2, size + cols, size), jnp.float32),
            pltpu.VMEM((2, size // BLOCK, BLOCK, BLOCK), jnp.float32),
        ],
        name="faces",
    )(schur_x, schur_y, far_x, far_y, res_x, res_y, far_res_x, far_res_y)


def coarse_kernel(rows, cols, unknowns, spots, links, loads, index, out, field_ref):
    count = rows * cols
    width = loads.shape[-1]
    line = cols * width
    total = count * width
    pad = loads.shape[1]
    spread = nn_dot_t(links[...], spots[...])
    take = lambda s, a: spread[(s * unknowns + a) * pad : (s * unknowns + a + 1) * pad, :]
    low_x = [take(0, a) for a in range(unknowns)]
    high_x = [move_lanes(take(1, a), -line) for a in range(unknowns)]
    low_y = [take(2, a) for a in range(unknowns)]
    high_y = [move_lanes(take(3, a), -width) for a in range(unknowns)]
    diagonal = spread[4 * unknowns * pad : 4 * unknowns * pad + pad, :]
    for part in low_x + high_x + low_y + high_y:
        diagonal = diagonal + jnp.abs(part)

    def operate(field):
        image = diagonal * field
        for group, by in ((low_x, line), (high_x, -line), (low_y, width), (high_y, -width)):
            near = move_lanes(field, by)
            for a in range(unknowns):
                image = image + group[a] * jnp.broadcast_to(near[a : a + 1, :], near.shape)
        return image

    def summed(values):
        line_sum = jnp.sum(values, axis=0, keepdims=True)
        wide = line_sum[:, :BLOCK]
        for at in range(BLOCK, total, BLOCK):
            wide = wide + line_sum[:, at : at + BLOCK]
        step = BLOCK // 2
        while step >= width:
            wide = wide + pltpu.roll(wide, step, 1)
            step //= 2
        wide = jnp.broadcast_to(wide, (pad, BLOCK))
        return jnp.concatenate([wide] * (total // BLOCK), axis=1)

    field = jnp.concatenate([loads[n] for n in range(count)], axis=1)
    coarse = jnp.zeros_like(field)
    remain = field
    direction = field
    norm_now = summed(remain * remain)
    def sweep(_, state):
        coarse, remain, direction, norm_now = state
        image = operate(direction)
        alpha = norm_now / summed(direction * image)
        coarse = coarse + alpha * direction
        remain = remain - alpha * image
        norm_next = summed(remain * remain)
        direction = remain + norm_next / norm_now * direction
        return coarse, remain, direction, norm_next

    coarse = lax.fori_loop(0, CITERS, sweep, (coarse, remain, direction, norm_now))[0]
    for at in range(total // BLOCK):
        field_ref[at] = coarse[:, at * BLOCK : (at + 1) * BLOCK]
    per = BLOCK // width
    mine = field_ref[index[0] // per]
    own = mine[:, :width]
    for s in range(1, per):
        own = jnp.where(index[0] % per == s, mine[:, s * width : (s + 1) * width], own)
    out[...] = own


def nn_dot_t(left, right):
    return lax.dot_general(
        left, right, (((0,), (0,)), ((), ())), precision=HIGH, preferred_element_type=jnp.float32
    )


def move_lanes(array, by):
    return pltpu.roll(array, by % array.shape[1], 1)


def coarse_solve(links, loads, rows, cols, unknowns, index):
    count, pad, width = loads.shape
    spots = jnp.repeat(jnp.eye(count, dtype=jnp.float32), width, axis=1)
    vmem = pl.BlockSpec(memory_space=pltpu.VMEM)
    return pl.pallas_call(
        lambda *refs: coarse_kernel(rows, cols, unknowns, *refs),
        in_specs=[vmem, vmem, vmem, pl.BlockSpec(memory_space=pltpu.SMEM)],
        out_specs=vmem,
        out_shape=jax.ShapeDtypeStruct((pad, width), jnp.float32),
        scratch_shapes=[pltpu.VMEM((count * width // BLOCK, pad, BLOCK), jnp.float32)],
        name="coarse",
    )(spots, links, loads, index)


def shards(
    schur_x, schur_y, residual_x, residual_y, basis_x, basis_y, couple_x, couple_y, coarse_shift
):
    row_index = lax.axis_index("sx")
    row_count = lax.axis_size("sx")
    col_index = lax.axis_index("sy")
    col_count = lax.axis_size("sy")
    far_y, far_res_y = shifted((schur_y[0, 0], residual_y[0, 0]), "sy", -1)
    far_x, far_res_x = shifted((schur_x[0, 0], residual_x[0, 0]), "sx", -1)

    unknowns = basis_x.shape[-2]
    pad = -(-unknowns // TILE) * TILE
    rhs_coarse = jnp.einsum("spf,srf->pr", basis_x[:, 0], residual_x[:, 0], precision=HIGH)
    rhs_coarse = rhs_coarse + jnp.einsum("spf,srf->pr", basis_y[0], residual_y[0], precision=HIGH)
    link_x = couple_x[0, 0] * (row_index > 0).astype(jnp.float32)
    link_y = couple_y[0, 0] * (col_index > 0).astype(jnp.float32)
    extra = pad - unknowns
    blocks = jnp.pad(jnp.stack([link_x, link_x.T, link_y, link_y.T]), ((0, 0), (0, 0), (0, extra)))
    packed = jnp.concatenate(
        [
            blocks.reshape(-1),
            jnp.pad(coarse_shift[0, 0], (0, extra)),
            jnp.pad(rhs_coarse, ((0, extra), (0, 0))).reshape(-1),
        ]
    )
    gathered = lax.all_gather(packed, ("sx", "sy"))
    split = 4 * unknowns * pad + pad
    links = gathered[:, :split]
    loads = gathered[:, split:].reshape(gathered.shape[0], pad, -1)
    index = (row_index * col_count + col_index).reshape(1)
    coarse = coarse_solve(links, loads, row_count, col_count, unknowns, index)[:unknowns]

    upper_x, upper_y = solve_faces(
        schur_x, schur_y, far_x, far_y, residual_x, residual_y, far_res_x, far_res_y
    )
    upper_x = jnp.where(row_index == row_count - 1, residual_x[1, 0], upper_x)
    upper_y = jnp.where(col_index == col_count - 1, residual_y[0, 1], upper_y)
    lower_x = shifted(upper_x, "sx", 1)
    lower_y = shifted(upper_y, "sy", 1)
    lower_x = jnp.where(row_index == 0, residual_x[0, 0], lower_x)
    lower_y = jnp.where(col_index == 0, residual_y[0, 0], lower_y)
    lift_x = jnp.einsum("pr,spf->srf", coarse, basis_x[:, 0], precision=HIGH)
    lift_y = jnp.einsum("pr,spf->srf", coarse, basis_y[0], precision=HIGH)
    out_x = (jnp.stack([lower_x, upper_x], axis=0) + lift_x)[:, None]
    out_y = (jnp.stack([lower_y, upper_y], axis=0) + lift_y)[None]
    return (out_x, out_y, coarse[None, None])


def solution(mesh):
    placed = (
        P("sx", "sy", None, None),
        P("sx", "sy", None, None),
        P("sx", "sy", None, None),
        P("sx", "sy", None, None),
        P("sx", "sy", None, None),
        P("sx", "sy", None, None),
        P("sx", "sy", None, None),
        P("sx", "sy", None, None),
        P("sx", "sy", None),
    )
    return jax.shard_map(
        shards,
        mesh=mesh,
        in_specs=placed,
        out_specs=(P("sx", "sy", None, None), P("sx", "sy", None, None), P("sx", "sy", None, None)),
        check_vma=False,
    )
```

```python
import jax
import jax.numpy as jnp
from jax import lax
from jax.experimental import pallas as pl
from jax.experimental.pallas import tpu as pltpu
from jax.sharding import PartitionSpec as P

CITERS = 8
TILE = 8
BLOCK = 128

HIGH = lax.Precision.HIGHEST


def nt_dot(left, right):
    return lax.dot_general(
        left, right, (((1,), (1,)), ((), ())), precision=HIGH, preferred_element_type=jnp.float32
    )


def nn_dot(left, right):
    return jnp.dot(left, right, precision=HIGH, preferred_element_type=jnp.float32)


def lane_spread(tile, k):
    return jnp.broadcast_to(tile[:, k : k + 1], tile.shape)


def row_spread(tile, k):
    return jnp.broadcast_to(tile[k : k + 1, :], tile.shape)


def inverse_factors(tiles):
    faces = range(len(tiles))
    tiles = [list(rows) for rows in tiles]
    count = len(tiles[0])
    shape = tiles[0][0].shape
    lane = lax.broadcasted_iota(jnp.int32, shape, 1)
    sub = lax.broadcasted_iota(jnp.int32, shape, 0)
    result = [[None] * count for _ in faces]
    for p in range(count):
        base = TILE * p
        cols = [[lane_spread(tiles[f][p], base + j) for j in range(TILE)] for f in faces]
        rows = [tiles[f][p] for f in faces]
        pivot_rows, pivots, inverses = {}, {}, {}
        for k in range(TILE):
            here = sub == k
            column = lane == base + k
            for f in faces:
                pivot = row_spread(cols[f][k], k)
                inverse = 1.0 / pivot
                pivot_row = jnp.where(column, 1.0, row_spread(rows[f], k))
                if k == 0:
                    pivot_rows[f], pivots[f], inverses[f] = pivot_row, pivot, inverse
                else:
                    later = sub >= k
                    pivot_rows[f] = jnp.where(later, pivot_row, pivot_rows[f])
                    pivots[f] = jnp.where(later, pivot, pivots[f])
                    inverses[f] = jnp.where(later, inverse, inverses[f])
                factor = jnp.where(here, 0.0, cols[f][k] * inverse)
                for j in range(k + 1, TILE):
                    cols[f][j] = cols[f][j] - factor * row_spread(cols[f][j], k)
                unit = jnp.where(here, 1.0, 0.0)
                rows[f] = jnp.where(column, unit, rows[f]) - factor * pivot_row
        for f in faces:
            scaled = pivot_rows[f] * lax.rsqrt(pivots[f])
            result[f][p] = jnp.where(lane <= base + sub, scaled, 0.0)
        inside = (lane >= base) & (lane < base + TILE)
        for f in faces:
            reduced = rows[f] * inverses[f]
            spread = [row_spread(reduced, j) for j in range(TILE)]
            for i in range(p + 1, count):
                tile = tiles[f][i]
                terms = [lane_spread(tile, base + j) * spread[j] for j in range(TILE)]
                while len(terms) > 1:
                    terms = [terms[t] + terms[t + 1] for t in range(0, len(terms), 2)]
                tiles[f][i] = jnp.where(inside, 0.0, tile) - terms[0]
    return result


def panel_rows(size):
    starts = [0]
    for k in range(size // BLOCK):
        starts.append(starts[-1] + size - k * BLOCK)
    return starts


def face_copies(block, residual, target, size, cols):
    starts = panel_rows(size)
    count = size // BLOCK
    pairs = []
    for k in range(count):
        lo = k * BLOCK
        at = target.at[starts[k] : starts[k + 1]]
        pairs.append((block.at[lo:size, lo : lo + BLOCK], at))
    for k in range(count):
        lo = k * BLOCK
        at = starts[count] + cols * k
        pairs.append((residual.at[:, lo : lo + BLOCK], target.at[at : at + cols]))
    return pairs


def pack_kernel(flags, schur_x, schur_y, res_x, res_y, out_x, out_y, sems):
    size = schur_x.shape[-1]
    cols = res_x.shape[-2]
    give = flags[1]
    pairs = face_copies(schur_y.at[0, give], res_y.at[0, give], out_y, size, cols)
    pairs += face_copies(schur_x.at[0, 0], res_x.at[0, 0], out_x, size, cols)
    copies = [pltpu.make_async_copy(src, dst, sems.at[n]) for n, (src, dst) in enumerate(pairs)]
    for copy in copies:
        copy.start()
    for copy in copies:
        copy.wait()


def pack_faces(flags, schur_x, schur_y, res_x, res_y):
    size = schur_x.shape[-1]
    cols = res_x.shape[-2]
    count = size // BLOCK
    rows = panel_rows(size)[-1] + cols * count
    shape = jax.ShapeDtypeStruct((rows, BLOCK), jnp.float32)
    anywhere = pl.BlockSpec(memory_space=pl.ANY)
    return pl.pallas_call(
        pack_kernel,
        in_specs=[pl.BlockSpec(memory_space=pltpu.SMEM)] + [anywhere] * 4,
        out_specs=[anywhere] * 2,
        out_shape=[shape, shape],
        scratch_shapes=[pltpu.SemaphoreType.DMA((4 * count,))],
        name="pack",
    )(flags, schur_x, schur_y, res_x, res_y)


def face_kernel(flags, schur_x, schur_y, far_x, far_y, res_x, res_y, out_x, out_y, *scratch):
    own, far, inv, own_sems, far_sems = scratch[:5]
    work = scratch[5:]
    size = schur_x.shape[-1]
    cols = res_x.shape[-2]
    count = size // BLOCK
    keep = flags[0]
    starts = panel_rows(size)
    sources = (
        (schur_x.at[1, 0], res_x.at[1, 0], far_x, out_x),
        (schur_y.at[0, keep], res_y.at[0, keep], far_y, out_y),
    )
    copies = []
    for f, (block, residual, other, _) in enumerate(sources):
        pairs = face_copies(block, residual, own.at[f], size, cols)
        mine = [
            pltpu.make_async_copy(src, dst, own_sems.at[f, n]) for n, (src, dst) in enumerate(pairs)
        ]
        spans = [(starts[k], starts[k + 1]) for k in range(count)]
        spans.append((starts[count], starts[count] + cols * count))
        theirs = [
            pltpu.make_async_copy(other.at[lo:hi], far.at[f, lo:hi], far_sems.at[f, n])
            for n, (lo, hi) in enumerate(spans)
        ]
        copies.append((mine, theirs))
    for k in range(count + 1):
        for mine, theirs in copies:
            for copy in mine[k : k + 1] if k < count else mine[count:]:
                copy.start()
            theirs[k].start()

    def arrive(k):
        for mine, theirs in copies:
            for copy in mine[k : k + 1] if k < count else mine[count:]:
                copy.wait()
            theirs[k].wait()

    def load(k):
        lo, hi = starts[k], starts[k + 1]
        for f in range(2):
            work[k][f, : hi - lo, :] = own[f, lo:hi, :] + far[f, lo:hi, :]

    def factor(k):
        tiles = [
            [work[k][f, TILE * i : TILE * i + TILE, :] for i in range(BLOCK // TILE)]
            for f in range(2)
        ]
        made = inverse_factors(tiles)
        for f in range(2):
            for i in range(BLOCK // TILE):
                inv[f, k, TILE * i : TILE * i + TILE, :] = made[f][i]

    for k in range(count + 1):
        arrive(k)
    for k in range(count):
        load(k)
    for f in range(2):
        sums = [None] * count
        for held in (own, far):
            pieces = [
                held[f, starts[count] + cols * k : starts[count] + cols * (k + 1), :]
                for k in range(count)
            ]
            for k in range(count):
                panel = held[f, starts[k] : starts[k + 1], :]
                across = jnp.concatenate(pieces[k:], axis=1)
                terms = {k: nn_dot(across, panel)}
                if k + 1 < count:
                    below = nt_dot(pieces[k], panel[BLOCK:])
                    for j in range(k + 1, count):
                        terms[j] = below[:, (j - k - 1) * BLOCK : (j - k) * BLOCK]
                for j, term in terms.items():
                    sums[j] = term if sums[j] is None else sums[j] + term
        for k in range(count):
            tall = size - k * BLOCK
            work[k][f, tall : tall + cols, :] = sums[k]

    for k in range(count):
        factor(k)
        for f in range(2):
            panel = nt_dot(work[k][f, BLOCK:, :], inv[f, k])
            work[k][f, BLOCK:, :] = panel
            for j in range(k + 1, count):
                at = (j - k - 1) * BLOCK
                work[j][f] = work[j][f] - nt_dot(panel[at:], panel[at : at + BLOCK])
    for f, (_, _, _, out) in enumerate(sources):
        solved = {}
        for k in reversed(range(count)):
            tall = size - k * BLOCK
            value = work[k][f, tall : tall + cols, :]
            for j in range(k + 1, count):
                at = (j - k) * BLOCK
                value = value - nn_dot(solved[j], work[k][f, at : at + BLOCK, :])
            solved[k] = nn_dot(value, inv[f, k])
            out[:, k * BLOCK : (k + 1) * BLOCK] = solved[k]


def solve_faces(flags, schur_x, schur_y, far_x, far_y, res_x, res_y):
    size = schur_x.shape[-1]
    cols = res_x.shape[-2]
    count = size // BLOCK
    anywhere = pl.BlockSpec(memory_space=pl.ANY)
    vmem = pl.BlockSpec(memory_space=pltpu.VMEM)
    shape = jax.ShapeDtypeStruct((cols, size), jnp.float32)
    return pl.pallas_call(
        face_kernel,
        in_specs=[pl.BlockSpec(memory_space=pltpu.SMEM)] + [anywhere] * 6,
        out_specs=[vmem, vmem],
        out_shape=[shape, shape],
        scratch_shapes=[
            pltpu.VMEM((2,) + far_x.shape, jnp.float32),
            pltpu.VMEM((2,) + far_x.shape, jnp.float32),
            pltpu.VMEM((2, count, BLOCK, BLOCK), jnp.float32),
            pltpu.SemaphoreType.DMA((2, 2 * count)),
            pltpu.SemaphoreType.DMA((2, count + 1)),
        ]
        + [pltpu.VMEM((2, size - k * BLOCK + cols, BLOCK), jnp.float32) for k in range(count)],
        name="faces",
    )(flags, schur_x, schur_y, far_x, far_y, res_x, res_y)


def move_lanes(array, by):
    return pltpu.roll(array, by % array.shape[1], 1)


def thirds(array):
    high = array.astype(jnp.bfloat16)
    rest = array - high.astype(jnp.float32)
    middle = rest.astype(jnp.bfloat16)
    return high, middle, (rest - middle.astype(jnp.float32)).astype(jnp.bfloat16)


def coarse_kernel(rows, cols, unknowns, width, flags, gathered, out, field_ref):
    count = rows * cols
    line = cols * width
    total = count * width
    pad = -(-unknowns // TILE) * TILE
    split = pad * width
    lane_home = lax.broadcasted_iota(jnp.int32, (count, total), 1) // width
    home = lane_home == lax.broadcasted_iota(jnp.int32, (count, total), 0)
    spots = jnp.where(home, 1.0, 0.0).astype(jnp.bfloat16)
    held = gathered[:, 0, :]
    pieces = thirds(held[:, split:])
    spread = 0.0
    for piece in pieces:
        spread = spread + lax.dot_general(
            piece, spots, (((0,), (0,)), ((), ())), preferred_element_type=jnp.float32
        )
    take = lambda s, a: spread[(s * unknowns + a) * pad : (s * unknowns + a + 1) * pad, :]
    low_x = [take(0, a) for a in range(unknowns)]
    high_x = [move_lanes(take(1, a), -line) for a in range(unknowns)]
    low_y = [take(2, a) for a in range(unknowns)]
    high_y = [move_lanes(take(3, a), -width) for a in range(unknowns)]
    diagonal = take(4, 0)
    for part in low_x + high_x + low_y + high_y:
        diagonal = diagonal + jnp.abs(part)

    def operate(field):
        image = diagonal * field
        for group, by in ((low_x, line), (high_x, -line), (low_y, width), (high_y, -width)):
            near = move_lanes(field, by)
            for a in range(unknowns):
                image = image + group[a] * jnp.broadcast_to(near[a : a + 1, :], near.shape)
        return image

    def summed(values):
        wide = values[:, :BLOCK]
        for at in range(BLOCK, total, BLOCK):
            wide = wide + values[:, at : at + BLOCK]
        wide = jnp.sum(wide, axis=0, keepdims=True)
        step = BLOCK // 2
        while step >= width:
            wide = wide + pltpu.roll(wide, step, 1)
            step //= 2
        wide = jnp.broadcast_to(wide, (pad, BLOCK))
        return jnp.concatenate([wide] * (total // BLOCK), axis=1)

    levels = []
    for b in range(pad):
        narrow = held[:, b * width : (b + 1) * width]
        wide = jnp.concatenate([narrow] * (BLOCK // width), axis=1)
        wide = jnp.concatenate([wide] * (total // BLOCK), axis=1)
        levels.append(jnp.sum(jnp.where(home, wide, 0.0), axis=0, keepdims=True))
    field = jnp.concatenate(levels, axis=0)

    def sweep(_, state):
        coarse, remain, direction, norm_now = state
        image = operate(direction)
        alpha = norm_now / summed(direction * image)
        coarse = coarse + alpha * direction
        remain = remain - alpha * image
        norm_next = summed(remain * remain)
        direction = remain + norm_next / norm_now * direction
        return coarse, remain, direction, norm_next

    state = (jnp.zeros_like(field), field, field, summed(field * field))
    coarse = lax.fori_loop(0, CITERS, sweep, state)[0]
    for at in range(total // BLOCK):
        field_ref[at] = coarse[:, at * BLOCK : (at + 1) * BLOCK]
    per = BLOCK // width
    place = flags[2]
    mine = field_ref[place // per]
    own = mine[:, :width]
    for s in range(1, per):
        own = jnp.where(place % per == s, mine[:, s * width : (s + 1) * width], own)
    out[...] = own


def coarse_solve(flags, gathered, rows, cols, unknowns, width):
    pad = -(-unknowns // TILE) * TILE
    vmem = pl.BlockSpec(memory_space=pltpu.VMEM)
    return pl.pallas_call(
        lambda *refs: coarse_kernel(rows, cols, unknowns, width, *refs),
        in_specs=[pl.BlockSpec(memory_space=pltpu.SMEM), vmem],
        out_specs=vmem,
        out_shape=jax.ShapeDtypeStruct((pad, width), jnp.float32),
        scratch_shapes=[pltpu.VMEM((rows * cols * width // BLOCK, pad, BLOCK), jnp.float32)],
        name="coarse",
    )(flags, gathered)


def finish_kernel(flags, solved_x, sent_x, solved_y, sent_y, res_x, res_y, basis_x, basis_y, coarse, out_x, out_y):
    keep, give = flags[0], flags[1]
    unknowns = basis_x.shape[1]
    weights = coarse[:unknowns, :]

    def lifted(basis):
        return lax.dot_general(
            weights, basis, (((0,), (0,)), ((), ())), precision=HIGH,
            preferred_element_type=jnp.float32,
        )

    out_x[1, 0] = jnp.where(flags[3] > 0, res_x[1, 0], solved_x[...]) + lifted(basis_x[1, :, 0, :])
    out_x[0, 0] = jnp.where(flags[4] > 0, res_x[0, 0], sent_x[...]) + lifted(basis_x[0, :, 0, :])
    mine = jnp.where(flags[5] > 0, res_y[0, keep], solved_y[...])
    other = jnp.where(flags[6] > 0, res_y[0, give], sent_y[...])
    out_y[0, 0] = jnp.where(keep == 0, mine, other) + lifted(basis_y[0, :, 0, :])
    out_y[0, 1] = jnp.where(keep == 1, mine, other) + lifted(basis_y[0, :, 1, :])


def finish(flags, solved_x, sent_x, solved_y, sent_y, res_x, res_y, basis_x, basis_y, coarse):
    vmem = pl.BlockSpec(memory_space=pltpu.VMEM)
    return pl.pallas_call(
        finish_kernel,
        in_specs=[pl.BlockSpec(memory_space=pltpu.SMEM)] + [vmem] * 9,
        out_specs=[vmem, vmem],
        out_shape=[
            jax.ShapeDtypeStruct(res_x.shape, jnp.float32),
            jax.ShapeDtypeStruct(res_y.shape, jnp.float32),
        ],
        name="finish",
    )(flags, solved_x, sent_x, solved_y, sent_y, res_x, res_y, basis_x, basis_y, coarse)


def shards(
    schur_x, schur_y, residual_x, residual_y, basis_x, basis_y, couple_x, couple_y, coarse_shift
):
    row = lax.axis_index("sx")
    rows = lax.axis_size("sx")
    col = lax.axis_index("sy")
    cols = lax.axis_size("sy")
    odd = row % 2
    keep, give = 1 - odd, odd
    ends_y = jnp.where(odd == 0, jnp.stack([col == cols - 1, col == 0]), jnp.stack([col == 0, col == cols - 1]))
    flags = jnp.stack(
        [keep, give, row * cols + col, row == rows - 1, row == 0, ends_y[0], ends_y[1]]
    ).astype(jnp.int32)
    pairs_y = []
    for i in range(rows):
        for j in range(cols):
            to = j + 1 if i % 2 else j - 1
            if 0 <= to < cols:
                pairs_y.append((i * cols + j, i * cols + to))
    pairs_x = [(i + 1, i) for i in range(rows - 1)]

    given_x, given_y = pack_faces(flags, schur_x, schur_y, residual_x, residual_y)
    far_y = lax.ppermute(given_y, ("sx", "sy"), pairs_y)
    far_x = lax.ppermute(given_x, "sx", pairs_x)

    unknowns = basis_x.shape[-2]
    width = residual_x.shape[-2]
    pad = -(-unknowns // TILE) * TILE
    extra = pad - unknowns
    rhs_coarse = jnp.einsum("spf,srf->pr", basis_x[:, 0], residual_x[:, 0], precision=HIGH)
    rhs_coarse = rhs_coarse + jnp.einsum("spf,srf->pr", basis_y[0], residual_y[0], precision=HIGH)
    link_x = couple_x[0, 0] * (row > 0).astype(jnp.float32)
    link_y = couple_y[0, 0] * (col > 0).astype(jnp.float32)
    blocks = jnp.pad(jnp.stack([link_x, link_x.T, link_y, link_y.T]), ((0, 0), (0, 0), (0, extra)))
    packed = jnp.concatenate(
        [
            jnp.pad(rhs_coarse, ((0, extra), (0, 0))).reshape(-1),
            blocks.reshape(-1),
            jnp.pad(coarse_shift[0, 0], (0, extra)),
        ]
    )
    packed = jnp.pad(packed, (0, -packed.shape[0] % BLOCK))
    copies = jnp.broadcast_to(packed, (rows * cols, 1, packed.shape[0]))
    gathered = lax.all_to_all(copies, ("sx", "sy"), 0, 0)

    solved_x, solved_y = solve_faces(
        flags, schur_x, schur_y, far_x, far_y, residual_x, residual_y
    )
    sent_x = lax.ppermute(solved_x, "sx", [(b, a) for a, b in pairs_x])
    sent_y = lax.ppermute(solved_y, ("sx", "sy"), [(b, a) for a, b in pairs_y])
    coarse = coarse_solve(flags, gathered, rows, cols, unknowns, width)
    turned_x = basis_x.transpose(0, 2, 1, 3)
    turned_y = basis_y.transpose(0, 2, 1, 3)
    out_x, out_y = finish(
        flags, solved_x, sent_x, solved_y, sent_y, residual_x, residual_y, turned_x, turned_y, coarse
    )
    return (out_x, out_y, coarse[None, None, :unknowns])


def solution(mesh):
    placed = (
        P("sx", "sy", None, None),
        P("sx", "sy", None, None),
        P("sx", "sy", None, None),
        P("sx", "sy", None, None),
        P("sx", "sy", None, None),
        P("sx", "sy", None, None),
        P("sx", "sy", None, None),
        P("sx", "sy", None, None),
        P("sx", "sy", None),
    )
    return jax.shard_map(
        shards,
        mesh=mesh,
        in_specs=placed,
        out_specs=(P("sx", "sy", None, None), P("sx", "sy", None, None), P("sx", "sy", None, None)),
        check_vma=False,
    )
```

```python
import jax
import jax.numpy as jnp
from jax import lax
from jax.experimental import pallas as pl
from jax.experimental.pallas import tpu as pltpu
from jax.sharding import PartitionSpec as P

CITERS = 8
TILE = 8
BLOCK = 128

HIGH = lax.Precision.HIGHEST


def nt_dot(left, right):
    return lax.dot_general(
        left, right, (((1,), (1,)), ((), ())), precision=HIGH, preferred_element_type=jnp.float32
    )


def nn_dot(left, right):
    return jnp.dot(left, right, precision=HIGH, preferred_element_type=jnp.float32)


def lane_spread(tile, k):
    return jnp.broadcast_to(tile[:, k : k + 1], tile.shape)


def row_spread(tile, k):
    return jnp.broadcast_to(tile[k : k + 1, :], tile.shape)


def inverse_factors(tiles):
    faces = range(len(tiles))
    tiles = [list(rows) for rows in tiles]
    count = len(tiles[0])
    shape = tiles[0][0].shape
    lane = lax.broadcasted_iota(jnp.int32, shape, 1)
    sub = lax.broadcasted_iota(jnp.int32, shape, 0)
    result = [[None] * count for _ in faces]
    for p in range(count):
        base = TILE * p
        cols = [[lane_spread(tiles[f][p], base + j) for j in range(TILE)] for f in faces]
        rows = [tiles[f][p] for f in faces]
        pivot_rows, pivots, inverses = {}, {}, {}
        for k in range(TILE):
            here = sub == k
            column = lane == base + k
            for f in faces:
                pivot = row_spread(cols[f][k], k)
                inverse = 1.0 / pivot
                pivot_row = jnp.where(column, 1.0, row_spread(rows[f], k))
                if k == 0:
                    pivot_rows[f], pivots[f], inverses[f] = pivot_row, pivot, inverse
                else:
                    later = sub >= k
                    pivot_rows[f] = jnp.where(later, pivot_row, pivot_rows[f])
                    pivots[f] = jnp.where(later, pivot, pivots[f])
                    inverses[f] = jnp.where(later, inverse, inverses[f])
                factor = jnp.where(here, 0.0, cols[f][k] * inverse)
                for j in range(k + 1, TILE):
                    cols[f][j] = cols[f][j] - factor * row_spread(cols[f][j], k)
                unit = jnp.where(here, 1.0, 0.0)
                rows[f] = jnp.where(column, unit, rows[f]) - factor * pivot_row
        for f in faces:
            scaled = pivot_rows[f] * lax.rsqrt(pivots[f])
            result[f][p] = jnp.where(lane <= base + sub, scaled, 0.0)
        inside = (lane >= base) & (lane < base + TILE)
        for f in faces:
            reduced = rows[f] * inverses[f]
            spread = [row_spread(reduced, j) for j in range(TILE)]
            for i in range(p + 1, count):
                tile = tiles[f][i]
                terms = [lane_spread(tile, base + j) * spread[j] for j in range(TILE)]
                while len(terms) > 1:
                    terms = [terms[t] + terms[t + 1] for t in range(0, len(terms), 2)]
                tiles[f][i] = jnp.where(inside, 0.0, tile) - terms[0]
    return result


def panel_rows(size):
    starts = [0]
    for k in range(size // BLOCK):
        starts.append(starts[-1] + size - k * BLOCK)
    return starts


def face_copies(block, residual, target, size, cols):
    starts = panel_rows(size)
    count = size // BLOCK
    pairs = []
    for k in range(count):
        lo = k * BLOCK
        at = target.at[starts[k] : starts[k + 1]]
        pairs.append((block.at[lo:size, lo : lo + BLOCK], at))
    for k in range(count):
        lo = k * BLOCK
        at = starts[count] + cols * k
        pairs.append((residual.at[:, lo : lo + BLOCK], target.at[at : at + cols]))
    return pairs


def y_sides():
    odd = lax.rem(lax.axis_index("sx"), 2)
    return 1 - odd, odd


def pack_kernel(schur_x, schur_y, res_x, res_y, out_x, out_y, sems):
    size = schur_x.shape[-1]
    cols = res_x.shape[-2]
    give = y_sides()[1]
    pairs = face_copies(schur_y.at[0, give], res_y.at[0, give], out_y, size, cols)
    pairs += face_copies(schur_x.at[0, 0], res_x.at[0, 0], out_x, size, cols)
    copies = [pltpu.make_async_copy(src, dst, sems.at[n]) for n, (src, dst) in enumerate(pairs)]
    for copy in copies:
        copy.start()
    for copy in copies:
        copy.wait()


def pack_faces(schur_x, schur_y, res_x, res_y):
    size = schur_x.shape[-1]
    cols = res_x.shape[-2]
    count = size // BLOCK
    rows = panel_rows(size)[-1] + cols * count
    shape = jax.ShapeDtypeStruct((rows, BLOCK), jnp.float32)
    anywhere = pl.BlockSpec(memory_space=pl.ANY)
    return pl.pallas_call(
        pack_kernel,
        in_specs=[anywhere] * 4,
        out_specs=[pl.BlockSpec(memory_space=pltpu.VMEM)] * 2,
        out_shape=[shape, shape],
        scratch_shapes=[pltpu.SemaphoreType.DMA((4 * count,))],
        name="pack",
    )(schur_x, schur_y, res_x, res_y)


def face_kernel(schur_x, schur_y, far_x, far_y, res_x, res_y, out_x, out_y, *scratch):
    own, inv, own_sems = scratch[:3]
    work = scratch[3:]
    far = (far_x, far_y)
    size = schur_x.shape[-1]
    cols = res_x.shape[-2]
    count = size // BLOCK
    keep = y_sides()[0]
    starts = panel_rows(size)
    sources = (
        (schur_x.at[1, 0], res_x.at[1, 0], out_x),
        (schur_y.at[0, keep], res_y.at[0, keep], out_y),
    )
    copies = []
    for f, (block, residual, _) in enumerate(sources):
        pairs = face_copies(block, residual, own.at[f], size, cols)
        copies.append(
            [pltpu.make_async_copy(src, dst, own_sems.at[f, n]) for n, (src, dst) in enumerate(pairs)]
        )
    for n in range(2 * count):
        for f in range(2):
            copies[f][n].start()
    for n in range(2 * count):
        for f in range(2):
            copies[f][n].wait()

    def load(k):
        lo, hi = starts[k], starts[k + 1]
        for f in range(2):
            work[k][f, : hi - lo, :] = own[f, lo:hi, :] + far[f][lo:hi, :]

    def factor(k):
        tiles = [
            [work[k][f, TILE * i : TILE * i + TILE, :] for i in range(BLOCK // TILE)]
            for f in range(2)
        ]
        made = inverse_factors(tiles)
        for f in range(2):
            for i in range(BLOCK // TILE):
                inv[f, k, TILE * i : TILE * i + TILE, :] = made[f][i]

    for k in range(count):
        load(k)
    for f in range(2):
        sums = [None] * count
        for held in (own.at[f], far[f]):
            pieces = [
                held[starts[count] + cols * k : starts[count] + cols * (k + 1), :]
                for k in range(count)
            ]
            for k in range(count):
                panel = held[starts[k] : starts[k + 1], :]
                across = jnp.concatenate(pieces[k:], axis=1)
                terms = {k: nn_dot(across, panel)}
                if k + 1 < count:
                    below = nt_dot(pieces[k], panel[BLOCK:])
                    for j in range(k + 1, count):
                        terms[j] = below[:, (j - k - 1) * BLOCK : (j - k) * BLOCK]
                for j, term in terms.items():
                    sums[j] = term if sums[j] is None else sums[j] + term
        for k in range(count):
            tall = size - k * BLOCK
            work[k][f, tall : tall + cols, :] = sums[k]

    for k in range(count):
        factor(k)
        for f in range(2):
            panel = nt_dot(work[k][f, BLOCK:, :], inv[f, k])
            work[k][f, BLOCK:, :] = panel
            for j in range(k + 1, count):
                at = (j - k - 1) * BLOCK
                work[j][f] = work[j][f] - nt_dot(panel[at:], panel[at : at + BLOCK])
    for f, (_, _, out) in enumerate(sources):
        solved = {}
        for k in reversed(range(count)):
            tall = size - k * BLOCK
            value = work[k][f, tall : tall + cols, :]
            for j in range(k + 1, count):
                at = (j - k) * BLOCK
                value = value - nn_dot(solved[j], work[k][f, at : at + BLOCK, :])
            solved[k] = nn_dot(value, inv[f, k])
            out[:, k * BLOCK : (k + 1) * BLOCK] = solved[k]


def solve_faces(schur_x, schur_y, far_x, far_y, res_x, res_y):
    size = schur_x.shape[-1]
    cols = res_x.shape[-2]
    count = size // BLOCK
    anywhere = pl.BlockSpec(memory_space=pl.ANY)
    vmem = pl.BlockSpec(memory_space=pltpu.VMEM)
    shape = jax.ShapeDtypeStruct((cols, size), jnp.float32)
    return pl.pallas_call(
        face_kernel,
        in_specs=[anywhere] * 2 + [vmem] * 2 + [anywhere] * 2,
        out_specs=[vmem, vmem],
        out_shape=[shape, shape],
        scratch_shapes=[
            pltpu.VMEM((2,) + far_x.shape, jnp.float32),
            pltpu.VMEM((2, count, BLOCK, BLOCK), jnp.float32),
            pltpu.SemaphoreType.DMA((2, 2 * count)),
        ]
        + [pltpu.VMEM((2, size - k * BLOCK + cols, BLOCK), jnp.float32) for k in range(count)],
        name="faces",
    )(schur_x, schur_y, far_x, far_y, res_x, res_y)


def move_lanes(array, by):
    return pltpu.roll(array, by % array.shape[1], 1)


def thirds(array):
    high = array.astype(jnp.bfloat16)
    rest = array - high.astype(jnp.float32)
    middle = rest.astype(jnp.bfloat16)
    return high, middle, (rest - middle.astype(jnp.float32)).astype(jnp.bfloat16)


def coarse_kernel(rows, cols, unknowns, width, gathered, out, field_ref):
    count = rows * cols
    line = cols * width
    total = count * width
    pad = -(-unknowns // TILE) * TILE
    split = pad * width
    lane_home = lax.broadcasted_iota(jnp.int32, (count, total), 1) // width
    home = lane_home == lax.broadcasted_iota(jnp.int32, (count, total), 0)
    spots = jnp.where(home, 1.0, 0.0).astype(jnp.bfloat16)
    held = gathered[:, 0, :]
    pieces = thirds(held[:, split:])
    spread = 0.0
    for piece in pieces:
        spread = spread + lax.dot_general(
            piece, spots, (((0,), (0,)), ((), ())), preferred_element_type=jnp.float32
        )
    take = lambda s, a: spread[(s * unknowns + a) * pad : (s * unknowns + a + 1) * pad, :]
    low_x = [take(0, a) for a in range(unknowns)]
    high_x = [move_lanes(take(1, a), -line) for a in range(unknowns)]
    low_y = [take(2, a) for a in range(unknowns)]
    high_y = [move_lanes(take(3, a), -width) for a in range(unknowns)]
    diagonal = take(4, 0)
    for part in low_x + high_x + low_y + high_y:
        diagonal = diagonal + jnp.abs(part)

    def operate(field):
        image = diagonal * field
        for group, by in ((low_x, line), (high_x, -line), (low_y, width), (high_y, -width)):
            near = move_lanes(field, by)
            for a in range(unknowns):
                image = image + group[a] * jnp.broadcast_to(near[a : a + 1, :], near.shape)
        return image

    def summed(values):
        wide = values[:, :BLOCK]
        for at in range(BLOCK, total, BLOCK):
            wide = wide + values[:, at : at + BLOCK]
        wide = jnp.sum(wide, axis=0, keepdims=True)
        step = BLOCK // 2
        while step >= width:
            wide = wide + pltpu.roll(wide, step, 1)
            step //= 2
        wide = jnp.broadcast_to(wide, (pad, BLOCK))
        return jnp.concatenate([wide] * (total // BLOCK), axis=1)

    levels = []
    for b in range(pad):
        narrow = held[:, b * width : (b + 1) * width]
        wide = jnp.concatenate([narrow] * (BLOCK // width), axis=1)
        wide = jnp.concatenate([wide] * (total // BLOCK), axis=1)
        levels.append(jnp.sum(jnp.where(home, wide, 0.0), axis=0, keepdims=True))
    field = jnp.concatenate(levels, axis=0)

    def sweep(_, state):
        coarse, remain, direction, norm_now = state
        image = operate(direction)
        alpha = norm_now / summed(direction * image)
        coarse = coarse + alpha * direction
        remain = remain - alpha * image
        norm_next = summed(remain * remain)
        direction = remain + norm_next / norm_now * direction
        return coarse, remain, direction, norm_next

    state = (jnp.zeros_like(field), field, field, summed(field * field))
    coarse = lax.fori_loop(0, CITERS, sweep, state)[0]
    for at in range(total // BLOCK):
        field_ref[at] = coarse[:, at * BLOCK : (at + 1) * BLOCK]
    per = BLOCK // width
    place = lax.axis_index("sx") * cols + lax.axis_index("sy")
    mine = field_ref[place // per]
    own = mine[:, :width]
    for s in range(1, per):
        own = jnp.where(place % per == s, mine[:, s * width : (s + 1) * width], own)
    out[...] = own


def coarse_solve(gathered, rows, cols, unknowns, width):
    pad = -(-unknowns // TILE) * TILE
    vmem = pl.BlockSpec(memory_space=pltpu.VMEM)
    return pl.pallas_call(
        lambda *refs: coarse_kernel(rows, cols, unknowns, width, *refs),
        in_specs=[vmem],
        out_specs=vmem,
        out_shape=jax.ShapeDtypeStruct((pad, width), jnp.float32),
        scratch_shapes=[pltpu.VMEM((rows * cols * width // BLOCK, pad, BLOCK), jnp.float32)],
        name="coarse",
    )(gathered)


def finish_kernel(
    solved_x, sent_x, solved_y, sent_y, res_x, res_y, basis_x, basis_y, coarse, out_x, out_y
):
    keep, give = y_sides()
    row, col = lax.axis_index("sx"), lax.axis_index("sy")
    last_row, last_col = lax.axis_size("sx") - 1, lax.axis_size("sy") - 1
    at_keep = jnp.where(keep == 1, col == last_col, col == 0)
    at_give = jnp.where(give == 1, col == last_col, col == 0)
    unknowns = basis_x.shape[1]
    weights = coarse[:unknowns, :]

    def lifted(basis):
        return lax.dot_general(
            weights, basis, (((0,), (0,)), ((), ())), precision=HIGH,
            preferred_element_type=jnp.float32,
        )

    out_x[1, 0] = jnp.where(row == last_row, res_x[1, 0], solved_x[...]) + lifted(basis_x[1, :, 0, :])
    out_x[0, 0] = jnp.where(row == 0, res_x[0, 0], sent_x[...]) + lifted(basis_x[0, :, 0, :])
    mine = jnp.where(at_keep, res_y[0, keep], solved_y[...])
    other = jnp.where(at_give, res_y[0, give], sent_y[...])
    out_y[0, 0] = jnp.where(keep == 0, mine, other) + lifted(basis_y[0, :, 0, :])
    out_y[0, 1] = jnp.where(keep == 1, mine, other) + lifted(basis_y[0, :, 1, :])


def finish(solved_x, sent_x, solved_y, sent_y, res_x, res_y, basis_x, basis_y, coarse):
    vmem = pl.BlockSpec(memory_space=pltpu.VMEM)
    return pl.pallas_call(
        finish_kernel,
        in_specs=[vmem] * 9,
        out_specs=[vmem, vmem],
        out_shape=[
            jax.ShapeDtypeStruct(res_x.shape, jnp.float32),
            jax.ShapeDtypeStruct(res_y.shape, jnp.float32),
        ],
        name="finish",
    )(solved_x, sent_x, solved_y, sent_y, res_x, res_y, basis_x, basis_y, coarse)


def shards(
    schur_x, schur_y, residual_x, residual_y, basis_x, basis_y, couple_x, couple_y, coarse_shift
):
    row = lax.axis_index("sx")
    rows = lax.axis_size("sx")
    col = lax.axis_index("sy")
    cols = lax.axis_size("sy")
    pairs_y = []
    for i in range(rows):
        for j in range(cols):
            to = j + 1 if i % 2 else j - 1
            if 0 <= to < cols:
                pairs_y.append((i * cols + j, i * cols + to))
    pairs_x = [(i + 1, i) for i in range(rows - 1)]

    given_x, given_y = pack_faces(schur_x, schur_y, residual_x, residual_y)
    far_y = lax.ppermute(given_y, ("sx", "sy"), pairs_y)
    far_x = lax.ppermute(given_x, "sx", pairs_x)

    unknowns = basis_x.shape[-2]
    width = residual_x.shape[-2]
    pad = -(-unknowns // TILE) * TILE
    extra = pad - unknowns
    rhs_coarse = jnp.einsum("spf,srf->pr", basis_x[:, 0], residual_x[:, 0], precision=HIGH)
    rhs_coarse = rhs_coarse + jnp.einsum("spf,srf->pr", basis_y[0], residual_y[0], precision=HIGH)
    link_x = couple_x[0, 0] * (row > 0).astype(jnp.float32)
    link_y = couple_y[0, 0] * (col > 0).astype(jnp.float32)
    blocks = jnp.pad(jnp.stack([link_x, link_x.T, link_y, link_y.T]), ((0, 0), (0, 0), (0, extra)))
    packed = jnp.concatenate(
        [
            jnp.pad(rhs_coarse, ((0, extra), (0, 0))).reshape(-1),
            blocks.reshape(-1),
            jnp.pad(coarse_shift[0, 0], (0, extra)),
        ]
    )
    packed = jnp.pad(packed, (0, -packed.shape[0] % BLOCK))
    copies = jnp.broadcast_to(packed, (rows * cols, 1, packed.shape[0]))
    gathered = lax.all_to_all(copies, ("sx", "sy"), 0, 0)

    near = lambda array: pltpu.with_memory_space_constraint(array, pltpu.VMEM)
    solved_x, solved_y = solve_faces(
        schur_x, schur_y, near(far_x), near(far_y), residual_x, residual_y
    )
    sent_x = lax.ppermute(solved_x, "sx", [(b, a) for a, b in pairs_x])
    sent_y = lax.ppermute(solved_y, ("sx", "sy"), [(b, a) for a, b in pairs_y])
    gathered = lax.optimization_barrier((gathered, solved_x))[0]
    coarse = coarse_solve(near(gathered), rows, cols, unknowns, width)
    turned_x = basis_x.transpose(0, 2, 1, 3)
    turned_y = basis_y.transpose(0, 2, 1, 3)
    out_x, out_y = finish(
        solved_x, near(sent_x), solved_y, near(sent_y), residual_x, residual_y, turned_x, turned_y, coarse
    )
    return (out_x, out_y, coarse[None, None, :unknowns])


def solution(mesh):
    placed = (
        P("sx", "sy", None, None),
        P("sx", "sy", None, None),
        P("sx", "sy", None, None),
        P("sx", "sy", None, None),
        P("sx", "sy", None, None),
        P("sx", "sy", None, None),
        P("sx", "sy", None, None),
        P("sx", "sy", None, None),
        P("sx", "sy", None),
    )
    return jax.shard_map(
        shards,
        mesh=mesh,
        in_specs=placed,
        out_specs=(P("sx", "sy", None, None), P("sx", "sy", None, None), P("sx", "sy", None, None)),
        check_vma=False,
    )
```

```python
import jax
import jax.numpy as jnp
from jax import lax
from jax.experimental import pallas as pl
from jax.experimental.pallas import tpu as pltpu
from jax.sharding import PartitionSpec as P

CITERS = 8
TILE = 8
BLOCK = 128
AHEAD = 1

HIGH = lax.Precision.HIGHEST


def nt_dot(left, right):
    return lax.dot_general(
        left, right, (((1,), (1,)), ((), ())), precision=HIGH, preferred_element_type=jnp.float32
    )


def nn_dot(left, right):
    return jnp.dot(left, right, precision=HIGH, preferred_element_type=jnp.float32)


def lane_spread(tile, k):
    index = jnp.full(tile.shape, k, jnp.int32)
    return jnp.take_along_axis(tile, index, axis=1, mode="promise_in_bounds")


def row_spread(tile, k):
    return jnp.broadcast_to(tile[k : k + 1, :], tile.shape)


def inverse_factors(tiles, tasks=()):
    faces = range(len(tiles))
    tiles = [list(rows) for rows in tiles]
    count = len(tiles[0])
    shape = tiles[0][0].shape
    lane = lax.broadcasted_iota(jnp.int32, shape, 1)
    sub = lax.broadcasted_iota(jnp.int32, shape, 0)
    result = [[None] * count for _ in faces]
    tasks = list(tasks)
    share = -(-len(tasks) // (count - 2))
    for p in range(count):
        base = TILE * p
        cols = [[lane_spread(tiles[f][p], base + j) for j in range(TILE)] for f in faces]
        rows = [tiles[f][p] for f in faces]
        pivot_rows, pivots, inverses = {}, {}, {}
        for k in range(TILE):
            here = sub == k
            column = lane == base + k
            for f in faces:
                pivot = row_spread(cols[f][k], k)
                inverse = 1.0 / pivot
                pivot_row = jnp.where(column, 1.0, row_spread(rows[f], k))
                if k == 0:
                    pivot_rows[f], pivots[f], inverses[f] = pivot_row, pivot, inverse
                else:
                    later = sub >= k
                    pivot_rows[f] = jnp.where(later, pivot_row, pivot_rows[f])
                    pivots[f] = jnp.where(later, pivot, pivots[f])
                    inverses[f] = jnp.where(later, inverse, inverses[f])
                factor = jnp.where(here, 0.0, cols[f][k] * inverse)
                for j in range(k + 1, TILE):
                    cols[f][j] = cols[f][j] - factor * row_spread(cols[f][j], k)
                unit = jnp.where(here, 1.0, 0.0)
                rows[f] = jnp.where(column, unit, rows[f]) - factor * pivot_row
        for f in faces:
            scaled = pivot_rows[f] * lax.rsqrt(pivots[f])
            result[f][p] = jnp.where(lane <= base + sub, scaled, 0.0)
        inside = (lane >= base) & (lane < base + TILE)
        for f in faces:
            reduced = rows[f] * inverses[f]
            spread = [row_spread(reduced, j) for j in range(TILE)]
            last = min(count, p + 1 + AHEAD)
            for i in range(p + 1, last):
                tile = tiles[f][i]
                terms = [lane_spread(tile, base + j) * spread[j] for j in range(TILE)]
                while len(terms) > 1:
                    terms = [terms[t] + terms[t + 1] for t in range(0, len(terms), 2)]
                tiles[f][i] = jnp.where(inside, 0.0, tile) - terms[0]
            if last < count:
                blank = jnp.zeros_like(reduced)
                placed = [reduced if i == p else blank for i in range(count)]
                below = nn_dot(jnp.concatenate(tiles[f][last:]), jnp.concatenate(placed))
                for i in range(last, count):
                    lo = TILE * (i - last)
                    tiles[f][i] = jnp.where(inside, 0.0, tiles[f][i]) - below[lo : lo + TILE]
        for task in tasks[:share]:
            task()
        tasks = tasks[share:]
    return result


def panel_rows(size):
    starts = [0]
    for k in range(size // BLOCK):
        starts.append(starts[-1] + size - k * BLOCK)
    return starts


def face_copies(block, residual, target, size, cols):
    starts = panel_rows(size)
    count = size // BLOCK
    pairs = []
    for k in range(count):
        lo = k * BLOCK
        at = target.at[starts[k] : starts[k + 1]]
        pairs.append((block.at[lo:size, lo : lo + BLOCK], at))
    for k in range(count):
        lo = k * BLOCK
        at = starts[count] + cols * k
        pairs.append((residual.at[:, lo : lo + BLOCK], target.at[at : at + cols]))
    return pairs


def y_sides():
    odd = lax.rem(lax.axis_index("sx"), 2)
    return 1 - odd, odd


def pack_kernel(schur_x, schur_y, res_x, res_y, out_y, out_x, sems):
    size = schur_x.shape[-1]
    cols = res_x.shape[-2]
    give = y_sides()[1]
    pairs = face_copies(schur_y.at[0, give], res_y.at[0, give], out_y, size, cols)
    pairs += face_copies(schur_x.at[0, 0], res_x.at[0, 0], out_x, size, cols)
    copies = [pltpu.make_async_copy(src, dst, sems.at[n]) for n, (src, dst) in enumerate(pairs)]
    for copy in copies:
        copy.start()
    for copy in copies:
        copy.wait()


def pack_faces(schur_x, schur_y, res_x, res_y):
    size = schur_x.shape[-1]
    cols = res_x.shape[-2]
    count = size // BLOCK
    rows = panel_rows(size)[-1] + cols * count
    shape = pltpu.VMEM((rows, BLOCK), jnp.float32)
    anywhere = pl.BlockSpec(memory_space=pl.ANY)
    return pl.pallas_call(
        pack_kernel,
        in_specs=[anywhere] * 4,
        out_specs=[pl.BlockSpec(memory_space=pltpu.VMEM)] * 2,
        out_shape=[shape, shape],
        scratch_shapes=[pltpu.SemaphoreType.DMA((4 * count,))],
        name="pack",
    )(schur_x, schur_y, res_x, res_y)


def face_kernel(schur_x, schur_y, far_x, far_y, res_x, res_y, out_x, out_y, *scratch):
    own, inv, own_sems = scratch[:3]
    work = scratch[3:]
    far = (far_x, far_y)
    size = schur_x.shape[-1]
    cols = res_x.shape[-2]
    count = size // BLOCK
    keep = y_sides()[0]
    starts = panel_rows(size)
    sources = (
        (schur_x.at[1, 0], res_x.at[1, 0], out_x),
        (schur_y.at[0, keep], res_y.at[0, keep], out_y),
    )
    copies = []
    for f, (block, residual, _) in enumerate(sources):
        pairs = face_copies(block, residual, own.at[f], size, cols)
        copies.append(
            [pltpu.make_async_copy(src, dst, own_sems.at[f, n]) for n, (src, dst) in enumerate(pairs)]
        )
    for n in range(2 * count):
        for f in range(2):
            copies[f][n].start()

    def load(f, k):
        lo, hi = starts[k], starts[k + 1]
        copies[f][k].wait()
        work[k][f, : hi - lo, :] = own[f, lo:hi, :] + far[f][lo:hi, :]

    def right_side(f, held, k):
        pieces = [
            held[starts[count] + cols * j : starts[count] + cols * (j + 1), :] for j in range(count)
        ]
        panel = held[starts[k] : starts[k + 1], :]
        sums[f][k].append(nn_dot(jnp.concatenate(pieces[k:], axis=1), panel))
        if k + 1 < count:
            below = nt_dot(pieces[k], panel[BLOCK:])
            for j in range(k + 1, count):
                sums[f][j].append(below[:, (j - k - 1) * BLOCK : (j - k) * BLOCK])

    def total_side(f):
        for k in range(count):
            tall = size - k * BLOCK
            total = sums[f][k][0]
            for term in sums[f][k][1:]:
                total = total + term
            work[k][f, tall : tall + cols, :] = total

    def factor(k, tasks):
        tiles = [
            [work[k][f, TILE * i : TILE * i + TILE, :] for i in range(BLOCK // TILE)]
            for f in range(2)
        ]
        made = inverse_factors(tiles, tasks)
        for f in range(2):
            for i in range(BLOCK // TILE):
                inv[f, k, TILE * i : TILE * i + TILE, :] = made[f][i]

    def rest_of_panel(f, k):
        work[k][f, 2 * BLOCK :, :] = nt_dot(work[k][f, 2 * BLOCK :, :], inv[f, k])

    def trailing(f, k, j):
        at = (j - k) * BLOCK
        skip = BLOCK if j == k + 1 else 0
        work[j][f, skip:, :] = work[j][f, skip:, :] - nt_dot(
            work[k][f, at + skip :, :], work[k][f, at : at + BLOCK, :]
        )

    sums = [[[] for _ in range(count)] for _ in range(2)]
    for f in range(2):
        load(f, 0)
    tasks = [lambda f=f, k=k: load(f, k) for k in range(1, count) for f in range(2)]
    for f in range(2):
        tasks.append(lambda f=f: [copy.wait() for copy in copies[f][count:]])
        for held in (far[f], own.at[f]):
            for k in range(count):
                tasks.append(lambda f=f, held=held, k=k: right_side(f, held, k))
        tasks.append(lambda f=f: total_side(f))
    for k in range(count):
        factor(k, tasks)
        if k + 1 == count:
            break
        for f in range(2):
            top = nt_dot(work[k][f, BLOCK : 2 * BLOCK, :], inv[f, k])
            work[k][f, BLOCK : 2 * BLOCK, :] = top
            work[k + 1][f, :BLOCK, :] = work[k + 1][f, :BLOCK, :] - nt_dot(top, top)
        tasks = [lambda f=f, k=k: rest_of_panel(f, k) for f in range(2)]
        tasks += [
            lambda f=f, k=k, j=j: trailing(f, k, j) for j in range(k + 1, count) for f in range(2)
        ]
    last = count - 1
    for f in range(2):
        work[last][f, BLOCK:, :] = nt_dot(work[last][f, BLOCK:, :], inv[f, last])
    solved = [{}, {}]
    for k in reversed(range(count)):
        tall = size - k * BLOCK
        for f, (_, _, out) in enumerate(sources):
            value = work[k][f, tall : tall + cols, :]
            for j in range(k + 1, count):
                at = (j - k) * BLOCK
                value = value - nn_dot(solved[f][j], work[k][f, at : at + BLOCK, :])
            solved[f][k] = nn_dot(value, inv[f, k])
            out[:, k * BLOCK : (k + 1) * BLOCK] = solved[f][k]


def solve_faces(schur_x, schur_y, far_x, far_y, res_x, res_y):
    size = schur_x.shape[-1]
    cols = res_x.shape[-2]
    count = size // BLOCK
    anywhere = pl.BlockSpec(memory_space=pl.ANY)
    vmem = pl.BlockSpec(memory_space=pltpu.VMEM)
    shape = pltpu.VMEM((cols, size), jnp.float32)
    return pl.pallas_call(
        face_kernel,
        in_specs=[anywhere] * 2 + [vmem] * 2 + [anywhere] * 2,
        out_specs=[vmem, vmem],
        out_shape=[shape, shape],
        scratch_shapes=[
            pltpu.VMEM((2,) + far_x.shape, jnp.float32),
            pltpu.VMEM((2, count, BLOCK, BLOCK), jnp.float32),
            pltpu.SemaphoreType.DMA((2, 2 * count)),
        ]
        + [pltpu.VMEM((2, size - k * BLOCK + cols, BLOCK), jnp.float32) for k in range(count)],
        name="faces",
    )(schur_x, schur_y, far_x, far_y, res_x, res_y)


def move_lanes(array, by):
    return pltpu.roll(array, by % array.shape[1], 1)


def thirds(array):
    high = array.astype(jnp.bfloat16)
    rest = array - high.astype(jnp.float32)
    middle = rest.astype(jnp.bfloat16)
    return high, middle, (rest - middle.astype(jnp.float32)).astype(jnp.bfloat16)


def coarse_kernel(
    rows, cols, unknowns, width, gathered, solved_x, solved_y, res_x, res_y, basis_x, basis_y,
    out, part_x, part_y, field_ref
):
    count = rows * cols
    line = cols * width
    total = count * width
    pad = -(-unknowns // TILE) * TILE
    split = pad * width
    lane_home = lax.broadcasted_iota(jnp.int32, (count, total), 1) // width
    home = lane_home == lax.broadcasted_iota(jnp.int32, (count, total), 0)
    spots = jnp.where(home, 1.0, 0.0).astype(jnp.bfloat16)
    held = gathered[:, 0, :]
    pieces = thirds(held[:, split:])
    spread = 0.0
    for piece in pieces:
        spread = spread + lax.dot_general(
            piece, spots, (((0,), (0,)), ((), ())), preferred_element_type=jnp.float32
        )
    take = lambda s, a: spread[(s * unknowns + a) * pad : (s * unknowns + a + 1) * pad, :]
    low_x = [take(0, a) for a in range(unknowns)]
    high_x = [move_lanes(take(1, a), -line) for a in range(unknowns)]
    low_y = [take(2, a) for a in range(unknowns)]
    high_y = [move_lanes(take(3, a), -width) for a in range(unknowns)]
    diagonal = take(4, 0)
    for part in low_x + high_x + low_y + high_y:
        diagonal = diagonal + jnp.abs(part)

    def operate(field):
        image = diagonal * field
        for group, by in ((low_x, line), (high_x, -line), (low_y, width), (high_y, -width)):
            near = move_lanes(field, by)
            for a in range(unknowns):
                image = image + group[a] * jnp.broadcast_to(near[a : a + 1, :], near.shape)
        return image

    def summed(values):
        wide = values[:, :BLOCK]
        for at in range(BLOCK, total, BLOCK):
            wide = wide + values[:, at : at + BLOCK]
        wide = jnp.sum(wide, axis=0, keepdims=True)
        step = BLOCK // 2
        while step >= width:
            wide = wide + pltpu.roll(wide, step, 1)
            step //= 2
        wide = jnp.broadcast_to(wide, (pad, BLOCK))
        return jnp.concatenate([wide] * (total // BLOCK), axis=1)

    levels = []
    for b in range(pad):
        narrow = held[:, b * width : (b + 1) * width]
        wide = jnp.concatenate([narrow] * (BLOCK // width), axis=1)
        wide = jnp.concatenate([wide] * (total // BLOCK), axis=1)
        levels.append(jnp.sum(jnp.where(home, wide, 0.0), axis=0, keepdims=True))
    field = jnp.concatenate(levels, axis=0)

    def sweep(_, state):
        coarse, remain, direction, norm_now = state
        image = operate(direction)
        alpha = norm_now / summed(direction * image)
        coarse = coarse + alpha * direction
        remain = remain - alpha * image
        norm_next = summed(remain * remain)
        direction = remain + norm_next / norm_now * direction
        return coarse, remain, direction, norm_next

    state = (jnp.zeros_like(field), field, field, summed(field * field))
    coarse = lax.fori_loop(0, CITERS, sweep, state)[0]
    for at in range(total // BLOCK):
        field_ref[at] = coarse[:, at * BLOCK : (at + 1) * BLOCK]
    per = BLOCK // width
    place = lax.axis_index("sx") * cols + lax.axis_index("sy")
    mine = field_ref[place // per]
    own = mine[:, :width]
    for s in range(1, per):
        own = jnp.where(place % per == s, mine[:, s * width : (s + 1) * width], own)
    own = own[:unknowns]
    out[0, :, 0, :] = own

    def lifted(basis):
        return nn_dot_t(own, basis)

    keep, give = y_sides()
    row, col = lax.axis_index("sx"), lax.axis_index("sy")
    keep_end = jnp.where(keep == 1, col == cols - 1, col == 0)
    give_end = jnp.where(give == 1, col == cols - 1, col == 0)
    mine_x = jnp.where(row == rows - 1, res_x[1, 0], solved_x[...])
    other_x = jnp.where(row == 0, res_x[0, 0], 0.0)
    mine_y = jnp.where(keep_end, res_y[0, keep], solved_y[...])
    other_y = jnp.where(give_end, res_y[0, give], 0.0)
    part_x[1, 0] = mine_x + lifted(basis_x[1, :, 0, :])
    part_x[0, 0] = other_x + lifted(basis_x[0, :, 0, :])
    part_y[0, 0] = jnp.where(keep == 0, mine_y, other_y) + lifted(basis_y[0, :, 0, :])
    part_y[0, 1] = jnp.where(keep == 1, mine_y, other_y) + lifted(basis_y[0, :, 1, :])


def nn_dot_t(left, right):
    return lax.dot_general(
        left, right, (((0,), (0,)), ((), ())), precision=HIGH, preferred_element_type=jnp.float32
    )


def coarse_solve(gathered, solved_x, solved_y, res_x, res_y, basis_x, basis_y, rows, cols):
    unknowns, width = basis_x.shape[1], res_x.shape[-2]
    pad = -(-unknowns // TILE) * TILE
    vmem = pl.BlockSpec(memory_space=pltpu.VMEM)
    return pl.pallas_call(
        lambda *refs: coarse_kernel(rows, cols, unknowns, width, *refs),
        in_specs=[vmem] * 7,
        out_specs=[vmem] * 3,
        out_shape=[
            jax.ShapeDtypeStruct((1, unknowns, 1, width), jnp.float32),
            pltpu.VMEM(res_x.shape, jnp.float32),
            pltpu.VMEM(res_y.shape, jnp.float32),
        ],
        scratch_shapes=[pltpu.VMEM((rows * cols * width // BLOCK, pad, BLOCK), jnp.float32)],
        name="coarse",
    )(gathered, solved_x, solved_y, res_x, res_y, basis_x, basis_y)


def finish_kernel(part_x, part_y, sent_x, sent_y, out_x, out_y):
    keep, give = y_sides()
    out_x[1] = part_x[1]
    out_x[0, 0] = part_x[0, 0] + sent_x[...]
    out_y[0, keep] = part_y[0, keep]
    out_y[0, give] = part_y[0, give] + sent_y[...]


def finish(part_x, part_y, sent_x, sent_y):
    vmem = pl.BlockSpec(memory_space=pltpu.VMEM)
    return pl.pallas_call(
        finish_kernel,
        in_specs=[vmem] * 4,
        out_specs=[vmem] * 2,
        out_shape=[
            jax.ShapeDtypeStruct(part_x.shape, jnp.float32),
            jax.ShapeDtypeStruct(part_y.shape, jnp.float32),
        ],
        name="finish",
    )(part_x, part_y, sent_x, sent_y)


def shards(
    schur_x, schur_y, residual_x, residual_y, basis_x, basis_y, couple_x, couple_y, coarse_shift
):
    row = lax.axis_index("sx")
    rows = lax.axis_size("sx")
    col = lax.axis_index("sy")
    cols = lax.axis_size("sy")
    pairs_y = []
    for i in range(rows):
        for j in range(cols):
            to = j + 1 if i % 2 else j - 1
            if 0 <= to < cols:
                pairs_y.append((i * cols + j, i * cols + to))
    pairs_x = [(i + 1, i) for i in range(rows - 1)]

    given_y, given_x = pack_faces(schur_x, schur_y, residual_x, residual_y)
    near = lambda array: pltpu.with_memory_space_constraint(array, pltpu.VMEM)
    far_y = lax.ppermute(near(given_y), ("sx", "sy"), pairs_y)
    far_x = lax.ppermute(near(given_x), "sx", pairs_x)

    unknowns = basis_x.shape[-2]
    width = residual_x.shape[-2]
    pad = -(-unknowns // TILE) * TILE
    extra = pad - unknowns
    rhs_coarse = jnp.einsum("spf,srf->pr", basis_x[:, 0], residual_x[:, 0], precision=HIGH)
    rhs_coarse = rhs_coarse + jnp.einsum("spf,srf->pr", basis_y[0], residual_y[0], precision=HIGH)
    link_x = couple_x[0, 0] * (row > 0).astype(jnp.float32)
    link_y = couple_y[0, 0] * (col > 0).astype(jnp.float32)
    blocks = jnp.pad(jnp.stack([link_x, link_x.T, link_y, link_y.T]), ((0, 0), (0, 0), (0, extra)))
    packed = jnp.concatenate(
        [
            jnp.pad(rhs_coarse, ((0, extra), (0, 0))).reshape(-1),
            blocks.reshape(-1),
            jnp.pad(coarse_shift[0, 0], (0, extra)),
        ]
    )
    packed = jnp.pad(packed, (0, -packed.shape[0] % BLOCK))
    copies = jnp.broadcast_to(packed, (rows * cols, 1, packed.shape[0]))
    gathered = lax.all_to_all(copies, ("sx", "sy"), 0, 0)

    solved_x, solved_y = solve_faces(
        schur_x, schur_y, near(far_x), near(far_y), residual_x, residual_y
    )
    sent_x = lax.ppermute(solved_x, "sx", [(b, a) for a, b in pairs_x])
    sent_y = lax.ppermute(solved_y, ("sx", "sy"), [(b, a) for a, b in pairs_y])
    gathered = lax.optimization_barrier((gathered, solved_x))[0]
    turned_x = basis_x.transpose(0, 2, 1, 3)
    turned_y = basis_y.transpose(0, 2, 1, 3)
    coarse, part_x, part_y = coarse_solve(
        near(gathered), near(solved_x), near(solved_y), residual_x, residual_y, turned_x, turned_y,
        rows, cols,
    )
    out_x, out_y = finish(near(part_x), near(part_y), near(sent_x), near(sent_y))
    return (out_x, out_y, coarse.transpose(0, 2, 1, 3))


def solution(mesh):
    placed = (
        P("sx", "sy", None, None),
        P("sx", "sy", None, None),
        P("sx", "sy", None, None),
        P("sx", "sy", None, None),
        P("sx", "sy", None, None),
        P("sx", "sy", None, None),
        P("sx", "sy", None, None),
        P("sx", "sy", None, None),
        P("sx", "sy", None),
    )
    return jax.shard_map(
        shards,
        mesh=mesh,
        in_specs=placed,
        out_specs=(P("sx", "sy", None, None), P("sx", "sy", None, None), P("sx", "sy", None, None)),
        check_vma=False,
    )
```

```python
import jax
import jax.numpy as jnp
from jax import lax
from jax.experimental import pallas as pl
from jax.experimental.pallas import tpu as pltpu
from jax.sharding import PartitionSpec as P


CITERS = 8
TILE = 8
BLOCK = 128
AHEAD = 1

HIGH = lax.Precision.HIGHEST


def nt_dot(left, right):
    return lax.dot_general(
        left, right, (((1,), (1,)), ((), ())), precision=HIGH, preferred_element_type=jnp.float32
    )


def nn_dot(left, right):
    return jnp.dot(left, right, precision=HIGH, preferred_element_type=jnp.float32)


def lane_spread(tile, k):
    index = jnp.full(tile.shape, k, jnp.int32)
    return jnp.take_along_axis(tile, index, axis=1, mode="promise_in_bounds")


def row_spread(tile, k):
    return jnp.broadcast_to(tile[k : k + 1, :], tile.shape)


def inverse_factors(tiles, tasks=()):
    faces = range(len(tiles))
    tiles = [list(rows) for rows in tiles]
    count = len(tiles[0])
    shape = tiles[0][0].shape
    lane = lax.broadcasted_iota(jnp.int32, shape, 1)
    sub = lax.broadcasted_iota(jnp.int32, shape, 0)
    result = [[None] * count for _ in faces]
    tasks = list(tasks)
    share = -(-len(tasks) // (count - 2))
    for p in range(count):
        base = TILE * p
        cols = [[lane_spread(tiles[f][p], base + j) for j in range(TILE)] for f in faces]
        rows = [tiles[f][p] for f in faces]
        pivot_rows, pivots, inverses = {}, {}, {}
        for k in range(TILE):
            here = sub == k
            column = lane == base + k
            for f in faces:
                pivot = row_spread(cols[f][k], k)
                inverse = 1.0 / pivot
                pivot_row = jnp.where(column, 1.0, row_spread(rows[f], k))
                if k == 0:
                    pivot_rows[f], pivots[f], inverses[f] = pivot_row, pivot, inverse
                else:
                    later = sub >= k
                    pivot_rows[f] = jnp.where(later, pivot_row, pivot_rows[f])
                    pivots[f] = jnp.where(later, pivot, pivots[f])
                    inverses[f] = jnp.where(later, inverse, inverses[f])
                factor = jnp.where(here, 0.0, cols[f][k] * inverse)
                for j in range(k + 1, TILE):
                    cols[f][j] = cols[f][j] - factor * row_spread(cols[f][j], k)
                unit = jnp.where(here, 1.0, 0.0)
                rows[f] = jnp.where(column, unit, rows[f]) - factor * pivot_row
        for f in faces:
            scaled = pivot_rows[f] * lax.rsqrt(pivots[f])
            result[f][p] = jnp.where(lane <= base + sub, scaled, 0.0)
        inside = (lane >= base) & (lane < base + TILE)
        for f in faces:
            reduced = rows[f] * inverses[f]
            spread = [row_spread(reduced, j) for j in range(TILE)]
            last = min(count, p + 1 + AHEAD)
            for i in range(p + 1, last):
                tile = tiles[f][i]
                terms = [lane_spread(tile, base + j) * spread[j] for j in range(TILE)]
                while len(terms) > 1:
                    terms = [terms[t] + terms[t + 1] for t in range(0, len(terms), 2)]
                tiles[f][i] = jnp.where(inside, 0.0, tile) - terms[0]
            if last < count:
                blank = jnp.zeros_like(reduced)
                placed = [reduced if i == p else blank for i in range(count)]
                below = nn_dot(jnp.concatenate(tiles[f][last:]), jnp.concatenate(placed))
                for i in range(last, count):
                    lo = TILE * (i - last)
                    tiles[f][i] = jnp.where(inside, 0.0, tiles[f][i]) - below[lo : lo + TILE]
        for task in tasks[:share]:
            task()
        tasks = tasks[share:]
    return result


def panel_rows(size):
    starts = [0]
    for k in range(size // BLOCK):
        starts.append(starts[-1] + size - k * BLOCK)
    return starts


def face_copies(block, residual, target, size, cols):
    starts = panel_rows(size)
    count = size // BLOCK
    pairs = []
    for k in range(count):
        lo = k * BLOCK
        at = target.at[starts[k] : starts[k + 1]]
        pairs.append((block.at[lo:size, lo : lo + BLOCK], at))
    for k in range(count):
        lo = k * BLOCK
        at = starts[count] + cols * k
        pairs.append((residual.at[:, lo : lo + BLOCK], target.at[at : at + cols]))
    return pairs


def y_sides():
    odd = lax.rem(lax.axis_index("sx"), 2)
    return 1 - odd, odd


def pack_kernel(schur_x, schur_y, res_x, res_y, out_x, out_y, sems):
    size = schur_x.shape[-1]
    cols = res_x.shape[-2]
    give = y_sides()[1]
    pairs = face_copies(schur_y.at[0, give], res_y.at[0, give], out_y, size, cols)
    pairs += face_copies(schur_x.at[0, 0], res_x.at[0, 0], out_x, size, cols)
    copies = [pltpu.make_async_copy(src, dst, sems.at[n]) for n, (src, dst) in enumerate(pairs)]
    for copy in copies:
        copy.start()
    for copy in copies:
        copy.wait()


def pack_faces(schur_x, schur_y, res_x, res_y):
    size = schur_x.shape[-1]
    cols = res_x.shape[-2]
    count = size // BLOCK
    rows = panel_rows(size)[-1] + cols * count
    shape = pltpu.VMEM((rows, BLOCK), jnp.float32)
    anywhere = pl.BlockSpec(memory_space=pl.ANY)
    return pl.pallas_call(
        pack_kernel,
        in_specs=[anywhere] * 4,
        out_specs=[pl.BlockSpec(memory_space=pltpu.VMEM)] * 2,
        out_shape=[shape, shape],
        scratch_shapes=[pltpu.SemaphoreType.DMA((4 * count,))],
        name="pack",
    )(schur_x, schur_y, res_x, res_y)


def face_kernel(schur_x, schur_y, far_x, far_y, res_x, res_y, out_x, out_y, *scratch):
    own, inv, own_sems = scratch[:3]
    work = scratch[3:]
    far = (far_x, far_y)
    size = schur_x.shape[-1]
    cols = res_x.shape[-2]
    count = size // BLOCK
    keep = y_sides()[0]
    starts = panel_rows(size)
    sources = (
        (schur_x.at[1, 0], res_x.at[1, 0], out_x),
        (schur_y.at[0, keep], res_y.at[0, keep], out_y),
    )
    copies = []
    for f, (block, residual, _) in enumerate(sources):
        pairs = face_copies(block, residual, own.at[f], size, cols)
        copies.append(
            [pltpu.make_async_copy(src, dst, own_sems.at[f, n]) for n, (src, dst) in enumerate(pairs)]
        )
    for n in range(2 * count):
        for f in range(2):
            copies[f][n].start()

    def load(f, k):
        lo, hi = starts[k], starts[k + 1]
        copies[f][k].wait()
        work[k][f, : hi - lo, :] = own[f, lo:hi, :] + far[f][lo:hi, :]

    def right_side(f, held, k):
        pieces = [
            held[starts[count] + cols * j : starts[count] + cols * (j + 1), :] for j in range(count)
        ]
        panel = held[starts[k] : starts[k + 1], :]
        sums[f][k].append(nn_dot(jnp.concatenate(pieces[k:], axis=1), panel))
        if k + 1 < count:
            below = nt_dot(pieces[k], panel[BLOCK:])
            for j in range(k + 1, count):
                sums[f][j].append(below[:, (j - k - 1) * BLOCK : (j - k) * BLOCK])

    def total_side(f):
        for k in range(count):
            tall = size - k * BLOCK
            total = sums[f][k][0]
            for term in sums[f][k][1:]:
                total = total + term
            work[k][f, tall : tall + cols, :] = total

    def factor(k, tasks):
        tiles = [
            [work[k][f, TILE * i : TILE * i + TILE, :] for i in range(BLOCK // TILE)]
            for f in range(2)
        ]
        made = inverse_factors(tiles, tasks)
        for f in range(2):
            for i in range(BLOCK // TILE):
                inv[f, k, TILE * i : TILE * i + TILE, :] = made[f][i]

    def rest_of_panel(f, k):
        work[k][f, 2 * BLOCK :, :] = nt_dot(work[k][f, 2 * BLOCK :, :], inv[f, k])

    def trailing(f, k, j):
        at = (j - k) * BLOCK
        skip = BLOCK if j == k + 1 else 0
        work[j][f, skip:, :] = work[j][f, skip:, :] - nt_dot(
            work[k][f, at + skip :, :], work[k][f, at : at + BLOCK, :]
        )

    sums = [[[] for _ in range(count)] for _ in range(2)]
    for f in range(2):
        load(f, 0)
    tasks = [lambda f=f, k=k: load(f, k) for k in range(1, count) for f in range(2)]
    for f in range(2):
        tasks.append(lambda f=f: [copy.wait() for copy in copies[f][count:]])
        for held in (far[f], own.at[f]):
            for k in range(count):
                tasks.append(lambda f=f, held=held, k=k: right_side(f, held, k))
        tasks.append(lambda f=f: total_side(f))
    for k in range(count):
        factor(k, tasks)
        if k + 1 == count:
            break
        for f in range(2):
            top = nt_dot(work[k][f, BLOCK : 2 * BLOCK, :], inv[f, k])
            work[k][f, BLOCK : 2 * BLOCK, :] = top
            work[k + 1][f, :BLOCK, :] = work[k + 1][f, :BLOCK, :] - nt_dot(top, top)
        tasks = [lambda f=f, k=k: rest_of_panel(f, k) for f in range(2)]
        tasks += [
            lambda f=f, k=k, j=j: trailing(f, k, j) for j in range(k + 1, count) for f in range(2)
        ]
    last = count - 1
    for f in range(2):
        work[last][f, BLOCK:, :] = nt_dot(work[last][f, BLOCK:, :], inv[f, last])
    solved = [{}, {}]
    for k in reversed(range(count)):
        tall = size - k * BLOCK
        for f, (_, _, out) in enumerate(sources):
            value = work[k][f, tall : tall + cols, :]
            for j in range(k + 1, count):
                at = (j - k) * BLOCK
                value = value - nn_dot(solved[f][j], work[k][f, at : at + BLOCK, :])
            solved[f][k] = nn_dot(value, inv[f, k])
            out[:, k * BLOCK : (k + 1) * BLOCK] = solved[f][k]


def solve_faces(schur_x, schur_y, far_x, far_y, res_x, res_y):
    size = schur_x.shape[-1]
    cols = res_x.shape[-2]
    count = size // BLOCK
    anywhere = pl.BlockSpec(memory_space=pl.ANY)
    vmem = pl.BlockSpec(memory_space=pltpu.VMEM)
    shape = pltpu.VMEM((cols, size), jnp.float32)
    return pl.pallas_call(
        face_kernel,
        in_specs=[anywhere] * 2 + [vmem] * 2 + [anywhere] * 2,
        out_specs=[vmem, vmem],
        out_shape=[shape, shape],
        scratch_shapes=[
            pltpu.VMEM((2,) + far_x.shape, jnp.float32),
            pltpu.VMEM((2, count, BLOCK, BLOCK), jnp.float32),
            pltpu.SemaphoreType.DMA((2, 2 * count)),
        ]
        + [pltpu.VMEM((2, size - k * BLOCK + cols, BLOCK), jnp.float32) for k in range(count)],
        name="faces",
    )(schur_x, schur_y, far_x, far_y, res_x, res_y)


def move_lanes(array, by):
    return pltpu.roll(array, by % array.shape[1], 1)


def thirds(array):
    high = array.astype(jnp.bfloat16)
    rest = array - high.astype(jnp.float32)
    middle = rest.astype(jnp.bfloat16)
    return high, middle, (rest - middle.astype(jnp.float32)).astype(jnp.bfloat16)


def coarse_kernel(
    rows, cols, unknowns, width, gathered, solved_x, solved_y, res_x, res_y, basis_x, basis_y,
    out, part_x, part_y, field_ref
):
    count = rows * cols
    line = cols * width
    total = count * width
    pad = -(-unknowns // TILE) * TILE
    split = pad * width
    lane_home = lax.broadcasted_iota(jnp.int32, (count, total), 1) // width
    home = lane_home == lax.broadcasted_iota(jnp.int32, (count, total), 0)
    spots = jnp.where(home, 1.0, 0.0).astype(jnp.bfloat16)
    held = gathered[:, 0, :]
    pieces = thirds(held[:, split:])
    spread = 0.0
    for piece in pieces:
        spread = spread + lax.dot_general(
            piece, spots, (((0,), (0,)), ((), ())), preferred_element_type=jnp.float32
        )
    take = lambda s, a: spread[(s * unknowns + a) * pad : (s * unknowns + a + 1) * pad, :]
    low_x = [take(0, a) for a in range(unknowns)]
    high_x = [move_lanes(take(1, a), -line) for a in range(unknowns)]
    low_y = [take(2, a) for a in range(unknowns)]
    high_y = [move_lanes(take(3, a), -width) for a in range(unknowns)]
    diagonal = take(4, 0)
    for part in low_x + high_x + low_y + high_y:
        diagonal = diagonal + jnp.abs(part)

    def operate(field):
        image = diagonal * field
        for group, by in ((low_x, line), (high_x, -line), (low_y, width), (high_y, -width)):
            near = move_lanes(field, by)
            for a in range(unknowns):
                image = image + group[a] * jnp.broadcast_to(near[a : a + 1, :], near.shape)
        return image

    def summed(values):
        wide = values[:, :BLOCK]
        for at in range(BLOCK, total, BLOCK):
            wide = wide + values[:, at : at + BLOCK]
        wide = jnp.sum(wide, axis=0, keepdims=True)
        step = BLOCK // 2
        while step >= width:
            wide = wide + pltpu.roll(wide, step, 1)
            step //= 2
        return jnp.broadcast_to(wide, (pad, BLOCK))

    def across(values):
        return jnp.concatenate([values] * (total // BLOCK), axis=1)

    levels = []
    for b in range(unknowns):
        narrow = held[:, b * width : (b + 1) * width]
        wide = jnp.concatenate([narrow] * (BLOCK // width), axis=1)
        wide = jnp.concatenate([wide] * (total // BLOCK), axis=1)
        levels.append(jnp.sum(jnp.where(home, wide, 0.0), axis=0, keepdims=True))
    levels += [jnp.zeros((1, total), jnp.float32)] * (pad - unknowns)
    field = jnp.concatenate(levels, axis=0)

    def sweep(_, state):
        coarse, remain, direction, norm_now = state
        image = operate(direction)
        alpha = across(norm_now / summed(direction * image))
        coarse = coarse + alpha * direction
        remain = remain - alpha * image
        norm_next = summed(remain * remain)
        direction = remain + across(norm_next / norm_now) * direction
        return coarse, remain, direction, norm_next

    state = (jnp.zeros_like(field), field, field, summed(field * field))
    coarse = lax.fori_loop(0, CITERS, sweep, state)[0]
    for at in range(total // BLOCK):
        field_ref[at] = coarse[:, at * BLOCK : (at + 1) * BLOCK]
    per = BLOCK // width
    place = lax.axis_index("sx") * cols + lax.axis_index("sy")
    mine = field_ref[place // per]
    own = mine[:, :width]
    for s in range(1, per):
        own = jnp.where(place % per == s, mine[:, s * width : (s + 1) * width], own)
    own = own[:unknowns]
    out[0, :, 0, :] = own

    def lifted(basis):
        return nn_dot_t(own, basis)

    keep, give = y_sides()
    row, col = lax.axis_index("sx"), lax.axis_index("sy")
    keep_end = jnp.where(keep == 1, col == cols - 1, col == 0)
    give_end = jnp.where(give == 1, col == cols - 1, col == 0)
    mine_x = jnp.where(row == rows - 1, res_x[1, 0], solved_x[...])
    other_x = jnp.where(row == 0, res_x[0, 0], 0.0)
    mine_y = jnp.where(keep_end, res_y[0, keep], solved_y[...])
    other_y = jnp.where(give_end, res_y[0, give], 0.0)
    part_x[1, 0] = mine_x + lifted(basis_x[1, :, 0, :])
    part_x[0, 0] = other_x + lifted(basis_x[0, :, 0, :])
    part_y[0, 0] = jnp.where(keep == 0, mine_y, other_y) + lifted(basis_y[0, :, 0, :])
    part_y[0, 1] = jnp.where(keep == 1, mine_y, other_y) + lifted(basis_y[0, :, 1, :])


def nn_dot_t(left, right):
    return lax.dot_general(
        left, right, (((0,), (0,)), ((), ())), precision=HIGH, preferred_element_type=jnp.float32
    )


def coarse_solve(gathered, solved_x, solved_y, res_x, res_y, basis_x, basis_y, rows, cols):
    unknowns, width = basis_x.shape[1], res_x.shape[-2]
    pad = -(-unknowns // TILE) * TILE
    vmem = pl.BlockSpec(memory_space=pltpu.VMEM)
    return pl.pallas_call(
        lambda *refs: coarse_kernel(rows, cols, unknowns, width, *refs),
        in_specs=[vmem] * 7,
        out_specs=[vmem] * 3,
        out_shape=[
            jax.ShapeDtypeStruct((1, unknowns, 1, width), jnp.float32),
            pltpu.VMEM(res_x.shape, jnp.float32),
            pltpu.VMEM(res_y.shape, jnp.float32),
        ],
        scratch_shapes=[pltpu.VMEM((rows * cols * width // BLOCK, pad, BLOCK), jnp.float32)],
        name="coarse",
    )(gathered, solved_x, solved_y, res_x, res_y, basis_x, basis_y)


def finish_kernel(part_x, part_y, sent_x, sent_y, out_x, out_y):
    keep, give = y_sides()
    out_x[1] = part_x[1]
    out_x[0, 0] = part_x[0, 0] + sent_x[...]
    out_y[0, keep] = part_y[0, keep]
    out_y[0, give] = part_y[0, give] + sent_y[...]


def finish(part_x, part_y, sent_x, sent_y):
    vmem = pl.BlockSpec(memory_space=pltpu.VMEM)
    return pl.pallas_call(
        finish_kernel,
        in_specs=[vmem] * 4,
        out_specs=[vmem] * 2,
        out_shape=[
            jax.ShapeDtypeStruct(part_x.shape, jnp.float32),
            jax.ShapeDtypeStruct(part_y.shape, jnp.float32),
        ],
        name="finish",
    )(part_x, part_y, sent_x, sent_y)


def shards(
    schur_x, schur_y, residual_x, residual_y, basis_x, basis_y, couple_x, couple_y, coarse_shift
):
    row = lax.axis_index("sx")
    rows = lax.axis_size("sx")
    col = lax.axis_index("sy")
    cols = lax.axis_size("sy")
    pairs_y = []
    for i in range(rows):
        for j in range(cols):
            to = j + 1 if i % 2 else j - 1
            if 0 <= to < cols:
                pairs_y.append((i * cols + j, i * cols + to))
    pairs_x = [(i + 1, i) for i in range(rows - 1)]

    given_x, given_y = pack_faces(schur_x, schur_y, residual_x, residual_y)
    near = lambda array: pltpu.with_memory_space_constraint(array, pltpu.VMEM)
    far_y = lax.ppermute(given_y, ("sx", "sy"), pairs_y)
    far_x = lax.ppermute(given_x, "sx", pairs_x)

    unknowns = basis_x.shape[-2]
    pad = -(-unknowns // TILE) * TILE
    extra = pad - unknowns
    rhs_coarse = jnp.einsum("spf,srf->pr", basis_x[:, 0], residual_x[:, 0], precision=HIGH)
    rhs_coarse = rhs_coarse + jnp.einsum("spf,srf->pr", basis_y[0], residual_y[0], precision=HIGH)
    link_x = couple_x[0, 0] * (row > 0).astype(jnp.float32)
    link_y = couple_y[0, 0] * (col > 0).astype(jnp.float32)
    blocks = jnp.pad(jnp.stack([link_x, link_x.T, link_y, link_y.T]), ((0, 0), (0, 0), (0, extra)))
    packed = jnp.concatenate(
        [
            jnp.pad(rhs_coarse, ((0, extra), (0, 0))).reshape(-1),
            blocks.reshape(-1),
            jnp.pad(coarse_shift[0, 0], (0, extra)),
        ]
    )
    packed = jnp.pad(packed, (0, -packed.shape[0] % BLOCK))
    copies = jnp.broadcast_to(packed, (rows * cols, 1, packed.shape[0]))
    gathered = lax.all_to_all(copies, ("sx", "sy"), 0, 0)

    solved_x, solved_y = solve_faces(
        schur_x, schur_y, near(far_x), near(far_y), residual_x, residual_y
    )
    sent_x = lax.ppermute(solved_x, "sx", [(b, a) for a, b in pairs_x])
    sent_y = lax.ppermute(solved_y, ("sx", "sy"), [(b, a) for a, b in pairs_y])
    gathered = lax.optimization_barrier((gathered, solved_x))[0]
    turned_x = basis_x.transpose(0, 2, 1, 3)
    turned_y = basis_y.transpose(0, 2, 1, 3)
    coarse, part_x, part_y = coarse_solve(
        near(gathered), near(solved_x), near(solved_y), residual_x, residual_y, turned_x, turned_y,
        rows, cols,
    )
    out_x, out_y = finish(near(part_x), near(part_y), near(sent_x), near(sent_y))
    return (out_x, out_y, coarse.transpose(0, 2, 1, 3))


def solution(mesh):
    placed = (
        P("sx", "sy", None, None),
        P("sx", "sy", None, None),
        P("sx", "sy", None, None),
        P("sx", "sy", None, None),
        P("sx", "sy", None, None),
        P("sx", "sy", None, None),
        P("sx", "sy", None, None),
        P("sx", "sy", None, None),
        P("sx", "sy", None),
    )
    return jax.shard_map(
        shards,
        mesh=mesh,
        in_specs=placed,
        out_specs=(P("sx", "sy", None, None), P("sx", "sy", None, None), P("sx", "sy", None, None)),
        check_vma=False,
    )
```
